256 devices in a mesh: grp: 4 (over x), seq: 16 (over z_hi, y, core), mdl: 4 (over z_lo).
Axes of the slice: x: 4, y: 4, z: 8 (z_hi: 2, z_lo: 4; z = z_hi * 4 + z_lo), core: 2. Of those that a mesh axis runs over, the one named last changes fastest.
Arguments:
- layer_input: bfloat16 [8192, 8192], P('seq', 'grp'), may hold values from -64 to 64
- attn_weight: bfloat16 [8192, 8, 1280], P(('grp', 'seq'), 'mdl'), may hold values from -0.0625 to 0.0625
- rate_weight: bfloat16 [8192, 64], P('grp', 'mdl'), may hold values from -0.15625 to 0.15625
- rate_bias: float32 [64], P(('mdl', 'grp')), may hold values from -8 to -3
- decay_rate: float32 [64], P(('mdl', 'grp')), may hold values from 1e-05 to 0.1
- skip_gain: float32 [64], P(('mdl', 'grp')), may hold values from 0.5 to 1.5
Outputs:
- teacher_heads: bfloat16 [8192, 8192], P('seq', ('mdl', 'grp'))
- student_heads: bfloat16 [8192, 8192], P('seq', ('mdl', 'grp'))
The draws below stay inside these ranges and needn't reach their ends.
All inputs are finite; a program needn't handle non-finite values.
Results may differ from the reference program's by a relative error of at most 0.03.
Values may be sent and summed in bfloat16 or wider, within the bound.
A program may use at most 192 MiB of HBM per device.

```python
import math
import jax
import jax.numpy as jnp
from jax import lax

D = 8192
HEADS = 64
KV_HEADS = 8
HEAD_DIM = 128
STRETCH = 256
TOKENS = 8192


def draw_layer_input(key, part):
    drawn = jax.random.normal(jax.random.fold_in(key, 105), (TOKENS, D), jnp.float32)
    return jnp.clip(drawn, -64.0, 64.0).astype(jnp.bfloat16)


def draw_decay_rate(key, part):
    unit = jax.random.uniform(jax.random.fold_in(key, 201), (HEADS,), jnp.float32)
    lower = math.log(0.0005)
    upper = math.log(0.1)
    return jnp.exp(lower + (upper - lower) * unit)


def levels(stream_key, extent, split, smallest, high):
    loudness, own = 1.0, jax.random.fold_in(stream_key, 6)
    for axis_at, shards_of in split:
        heights = jnp.exp(jax.random.uniform(jax.random.fold_in(own, axis_at), (shards_of,), jnp.float32, smallest / len(split), high / len(split)))
        loudness = loudness * jnp.repeat(heights, extent[axis_at] // shards_of).reshape([-1 if axis == axis_at else 1 for axis in range(len(extent))])
    return loudness


def bell_draw(own_key, dims, width, reach, split=(), kind=jnp.bfloat16):
    result = jax.random.normal(own_key, dims, jnp.float32) * width
    if len(split) > 0:
        result = levels(own_key, dims, split, -0.22, 0.18) * result
    return jnp.clip(result, min=-reach, max=reach).astype(kind)


def setup_inputs(seed: int = 0) -> dict:
    key_list = jax.random.split(jax.random.key(seed), 7)
    return {
        "layer_input": draw_layer_input(jax.random.fold_in(key_list[6], 71), 0),
        "attn_weight": bell_draw(key_list[1], (D, KV_HEADS, (HEADS // KV_HEADS + 2) * HEAD_DIM), D ** -0.5, 0.0625, ((0, 64), (1, 4))),
        "rate_weight": bell_draw(key_list[2], (D, HEADS), (D // 6) ** -0.5, 0.15625, ((0, 4), (1, 4))),
        "rate_bias": jnp.clip(-8.0 + 5.0 * jax.random.uniform(key_list[3], (HEADS,), jnp.float32) ** levels(key_list[3], (HEADS,), ((0, 16),), -0.2, 0.2), -8.0, -3.0),
        "decay_rate": draw_decay_rate(jax.random.fold_in(key_list[6], 71), 0),
        "skip_gain": jnp.clip(0.5 + 1.0 * jax.random.uniform(key_list[5], (HEADS,), jnp.float32) ** levels(key_list[5], (HEADS,), ((0, 16),), -0.2, 0.2), 0.5, 1.5),
    }


ROPE_BASE = 500000.0


def rope_angles(positions):
    half = HEAD_DIM // 2
    freq = ROPE_BASE ** (-2.0 * jnp.arange(half, dtype=jnp.float32) / HEAD_DIM)
    angle = positions.astype(jnp.float32)[:, None] * freq[None, :]
    return jnp.cos(angle), jnp.sin(angle)


def rotate(vectors, cosine, sine):
    half = vectors.shape[-1] // 2
    first = vectors[..., :half]
    second = vectors[..., half:]
    cosine = cosine[:, None, :]
    sine = sine[:, None, :]
    return jnp.concatenate([first * cosine - second * sine, second * cosine + first * sine], axis=-1)


def attend_head(query, keys, values, scale):
    block = math.gcd(512, TOKENS)
    pieces = []
    for first in range(0, TOKENS, block):
        last = first + block
        scores = jnp.dot(query[first:last], keys[:last].T, preferred_element_type=jnp.float32) * scale
        rows = jnp.arange(first, last, dtype=jnp.int32)[:, None]
        cols = jnp.arange(last, dtype=jnp.int32)[None, :]
        causal = cols <= rows
        masked = jnp.where(causal, scores, -1e30)
        top = jnp.max(masked, axis=1, keepdims=True)
        weights = jnp.where(causal, jnp.exp(masked - top), 0.0)
        total = jnp.sum(weights, axis=1, keepdims=True)
        numer = jnp.dot(weights.astype(jnp.bfloat16), values[:last], preferred_element_type=jnp.float32)
        pieces.append((numer / total).astype(jnp.bfloat16))
    return jnp.concatenate(pieces, axis=0)


def student_scan(cterm, bterm, values, raw, rate_bias, decay_rate, skip_gain, scale):
    group = HEADS // KV_HEADS
    step = jax.nn.softplus(raw + rate_bias[None, :])
    log_decay = -decay_rate[None, :] * step
    b_all = jnp.repeat(bterm, group, axis=1)
    x_all = jnp.repeat(values, group, axis=1)
    count = TOKENS // STRETCH

    def stretched(array):
        return array.reshape((count, STRETCH) + array.shape[1:])

    causal = (jnp.arange(STRETCH, dtype=jnp.int32)[:, None] >= jnp.arange(STRETCH, dtype=jnp.int32)[None, :])[None]

    def advance(state, parts):
        cpart, bpart, xpart, decay, rate = parts
        cfull = cpart.astype(jnp.float32)
        bfull = bpart.astype(jnp.float32)
        xfull = xpart.astype(jnp.float32)
        cum = jnp.cumsum(decay, axis=0)
        gram = jnp.einsum('thn,shn->hts', cfull, bfull, precision=lax.Precision.HIGHEST) * scale
        diff = cum.T[:, :, None] - cum.T[:, None, :]
        mix = jnp.where(causal, jnp.exp(jnp.where(causal, diff, -1e4)) * rate.T[:, None, :] * gram, 0.0)
        mix = mix.astype(jnp.bfloat16).astype(jnp.float32)
        intra = jnp.einsum('hts,shp->thp', mix, xfull, precision=lax.Precision.HIGHEST)
        carried = jnp.einsum('thn,hnp->thp', cfull, state, precision=lax.Precision.HIGHEST) * scale * jnp.exp(cum)[:, :, None]
        weighted = ((jnp.exp(cum[-1][None, :] - cum) * rate)[:, :, None] * bfull).astype(jnp.bfloat16).astype(jnp.float32)
        contribution = jnp.einsum('shn,shp->hnp', weighted, xfull, precision=lax.Precision.HIGHEST)
        state = jnp.exp(cum[-1])[:, None, None] * state + contribution
        output = (intra + carried + skip_gain[None, :, None] * xfull).astype(jnp.bfloat16)
        return state, output

    start = jnp.zeros((HEADS, HEAD_DIM, HEAD_DIM), jnp.float32)
    _, outputs = lax.scan(advance, start, (stretched(cterm), stretched(b_all), stretched(x_all), stretched(log_decay), stretched(step)))
    return outputs.reshape(TOKENS, HEADS * HEAD_DIM)


def reference(layer_input, attn_weight, rate_weight, rate_bias, decay_rate, skip_gain):
    group = HEADS // KV_HEADS
    scale = HEAD_DIM ** -0.5
    merged = jnp.dot(layer_input, attn_weight.reshape(D, KV_HEADS * (group + 2) * HEAD_DIM), preferred_element_type=jnp.float32)
    merged = merged.reshape(TOKENS, KV_HEADS, group + 2, HEAD_DIM)
    query = merged[:, :, :group].reshape(TOKENS, HEADS, HEAD_DIM)
    keys = merged[:, :, group]
    values = merged[:, :, group + 1].astype(jnp.bfloat16)
    raw = jnp.dot(layer_input, rate_weight, preferred_element_type=jnp.float32)
    cosine, sine = rope_angles(jnp.arange(TOKENS, dtype=jnp.int32))
    rot_query = rotate(query, cosine, sine).astype(jnp.bfloat16)
    rot_keys = rotate(keys, cosine, sine).astype(jnp.bfloat16)

    def one_head(index):
        kv_index = index // group
        return attend_head(rot_query[:, index], rot_keys[:, kv_index], values[:, kv_index], scale)

    heads = lax.map(one_head, jnp.arange(HEADS, dtype=jnp.int32))
    teacher_heads = jnp.transpose(heads, (1, 0, 2)).reshape(TOKENS, HEADS * HEAD_DIM)
    student_heads = student_scan(query.astype(jnp.bfloat16), keys.astype(jnp.bfloat16), values, raw, rate_bias, decay_rate, skip_gain, scale)
    return teacher_heads, student_heads
```

```python
import functools
import math

import jax
import jax.numpy as jnp
import numpy as np
from jax import lax
from jax.experimental import pallas as pl
from jax.experimental.pallas import tpu as pltpu
from jax.sharding import PartitionSpec as P

HEAD_DIM = 128
STRETCH = 256
ROPE_BASE = 500000.0
FAR_BELOW = -1e30
TOK = 512
LOCAL_HEADS = 4
CHUNKS = 5
COPIES = 11
SCALE = HEAD_DIM**-0.5
LOG2E = math.log2(math.e)
MESH = pl.DeviceIdType.MESH
BF = jnp.bfloat16
F32 = jnp.float32


def places():
    g, s, m = lax.axis_index("grp"), lax.axis_index("seq"), lax.axis_index("mdl")
    zh, y, c = s // 8, (s // 2) % 4, s % 2

    def seq(zh, y, c):
        return zh * 8 + y * 2 + c

    up, down, far = lax.rem(y + 1, 4), lax.rem(y + 3, 4), lax.rem(y + 2, 4)
    return {
        "g": g, "s": s, "zh": zh, "y": y, "c": c,
        "zy": zh * 4 + y,
        "up": up, "down": down, "far": far,
        "R": (g, seq(zh, up, c), m),
        "L": (g, seq(zh, down, c), m),
        "Z": (g, seq(1 - zh, y, c), m),
        "S": (g, seq(zh, y, 1 - c), m),
        "G": [(lax.rem(g + d, 4), s, m) for d in (1, 2, 3)],
    }


def enter(names, p):
    bar = pltpu.get_barrier_semaphore()
    targets = []
    for name in names:
        targets += p[name] if name == "G" else [p[name]]
    for dev in targets:
        pl.semaphore_signal(bar, inc=1, device_id=dev, device_id_type=MESH)
    pl.semaphore_wait(bar, len(targets))


class Gather:
    def __init__(self, buf, ssem, rsem, p, half, up_only):
        self.buf, self.ssem, self.rsem, self.p = buf, ssem, rsem, p
        self.rows = buf.shape[-2]
        self.half, self.up_only = half, up_only

    def copy(self, k, dev, zy, first=None, count=None, core=None):
        c = self.p["c"] if core is None else core
        ref = self.buf.at[c, zy] if first is None else self.buf.at[c, zy, pl.ds(first, count)]
        return pltpu.make_async_remote_copy(
            src_ref=ref, dst_ref=ref, send_sem=self.ssem.at[k], recv_sem=self.rsem.at[k],
            device_id=dev, device_id_type=MESH,
        )

    def four(self, k, zh, core):
        ref = self.buf.at[core, pl.ds(zh * 4, 4)]
        return pltpu.make_async_remote_copy(
            src_ref=ref, dst_ref=ref, send_sem=self.ssem.at[k], recv_sem=self.rsem.at[k],
            device_id=self.p["S"], device_id_type=MESH,
        )

    def only(self, cond, f):
        if self.up_only:
            pl.when(cond)(f)
        else:
            f()

    def base(self, own):
        return (self.p["zh"] if own else 1 - self.p["zh"]) * 4

    def spread(self, own):
        p, k = self.p, 0 if own else 5
        at = self.base(own) + p["y"]
        return self.copy(k, p["R"], at), self.copy(k + 1, p["L"], at)

    def arrive(self, own):
        p, k = self.p, 0 if own else 5
        return (
            self.copy(k, p["R"], self.base(own) + p["down"]),
            self.copy(k + 1, p["L"], self.base(own) + p["up"]),
        )

    def forward(self, own):
        p, k = self.p, 2 if own else 7
        return (
            self.copy(k, p["R"], self.base(own) + p["down"], 0, self.half),
            self.copy(k + 1, p["L"], self.base(own) + p["up"], self.half, self.rows - self.half),
        )

    def halves(self, own):
        p, k = self.p, 2 if own else 7
        return (
            self.copy(k, p["R"], self.base(own) + p["far"], 0, self.half),
            self.copy(k + 1, p["L"], self.base(own) + p["far"], self.half, self.rows - self.half),
        )

    def a(self):
        right, left = self.spread(True)
        right.start()
        left.start()
        self.only(self.p["zh"] == 0, lambda: self.copy(4, self.p["Z"], self.p["zy"]).start())

    def pass_on(self, own):
        for got, on in zip(self.arrive(own), self.forward(own)):
            got.wait_recv()
            on.start()

    def b(self):
        self.pass_on(True)

        def other():
            self.copy(4, self.p["Z"], self.base(False) + self.p["y"]).wait_recv()
            for cp in self.spread(False):
                cp.start()

        self.only(self.p["zh"] == 1, other)

    def finish(self, own):
        for cp in self.halves(own):
            cp.wait_recv()
        self.four(9 if own else 10, self.p["zh"] if own else 1 - self.p["zh"], self.p["c"]).start()

    def c(self):
        self.finish(True)
        self.only(self.p["zh"] == 1, lambda: self.pass_on(False))

    def d(self):
        self.only(self.p["zh"] == 1, lambda: self.finish(False))

    def e(self):
        self.four(9, self.p["zh"], 1 - self.p["c"]).wait_recv()
        self.only(
            self.p["zh"] == 1, lambda: self.four(10, 1 - self.p["zh"], 1 - self.p["c"]).wait_recv()
        )

    def sent(self):
        for cp in (*self.spread(True), *self.forward(True)):
            cp.wait_send()
        self.only(self.p["zh"] == 0, lambda: self.copy(4, self.p["Z"], self.p["zy"]).wait_send())

        def other():
            for cp in (*self.spread(False), *self.forward(False)):
                cp.wait_send()
            self.four(10, 1 - self.p["zh"], self.p["c"]).wait_send()

        self.only(self.p["zh"] == 1, other)
        self.four(9, self.p["zh"], self.p["c"]).wait_send()


def dot(a, b):
    return jnp.dot(a, b, preferred_element_type=F32)


def dot_t(a, b, precision=None):
    return lax.dot_general(
        a, b, (((1,), (1,)), ((), ())), preferred_element_type=F32, precision=precision
    )


def project_kernel(
    x_ref, w_ref, rate_ref, near_ref, base_ref,
    rq_ref, ct_ref, kv_ref, b_ref, raw_ref,
    wg, xp, own, qsend, qrecv, kvsend, kvrecv, rawsend, rawrecv,
    wssem, wrsem, gssem, grsem,
):
    p = places()
    g = p["g"]

    def place(chunk):
        for d in range(4):
            k = d // 2
            first = k * 1280 + (1024 + (d % 2) * 128 if chunk == 0 else (d % 2) * 512 + (chunk - 1) * 128)
            wg[chunk, p["c"], p["zy"], :, d * 128 : d * 128 + 128] = w_ref[:, first : first + 128]

    gathers = [
        Gather(wg.at[n], wssem.at[n], wrsem.at[n], p, 64, False) for n in range(CHUNKS)
    ]
    place(0)
    enter(["R", "L", "Z", "S", "G"], p)
    gathers[0].a()
    place(1)
    gathers[1].a()
    for n in range(2, CHUNKS):
        place(n)

    def tile(source, target, k, d):
        return pltpu.make_async_remote_copy(
            src_ref=source, dst_ref=target, send_sem=gssem.at[k, d], recv_sem=grsem.at[k, d],
            device_id=p["G"][d], device_id_type=MESH,
        )

    def raw_tile(d):
        return tile(rawsend.at[lax.rem(g + d + 1, 4)], rawrecv.at[d], CHUNKS, d)

    def kv_tile(d):
        return tile(kvsend.at[lax.rem(g + d + 1, 4) // 2], kvrecv.at[d], 0, d)

    def q_tile(n, d):
        return tile(qsend.at[n - 1, lax.rem(g + d + 1, 4)], qrecv.at[n - 1, d], n, d)

    def tiles(n):
        return [kv_tile(d) if n == 0 else q_tile(n, d) for d in range(3)]

    raw = dot_t(rate_ref[...], x_ref[...])
    for d in range(4):
        rawsend[d] = jnp.concatenate([raw[4 * d : 4 * d + 4], raw[4 * d : 4 * d + 4]], axis=0)
    for d in range(3):
        raw_tile(d).start()
    for core in range(2):
        for zy in range(8):
            src = (zy * 2 + core) * 128
            xp[core, :, zy * 128 : zy * 128 + 128] = x_ref[:, src : src + 128]

    def angles():
        near_c, near_s = near_ref[0], near_ref[1]
        far_c, far_s = base_ref[0, pl.ds(p["s"], 1), :], base_ref[1, pl.ds(p["s"], 1), :]
        sign = jnp.where(lax.broadcasted_iota(jnp.int32, (1, HEAD_DIM), 1) < HEAD_DIM // 2, -1.0, 1.0)
        cosine = near_c * far_c - near_s * far_s
        sine = (near_s * far_c + near_c * far_s) * sign
        return cosine, sine

    def rotate(u):
        cosine, sine = angles()
        return u * cosine + pltpu.roll(u, HEAD_DIM // 2, 1) * sine

    def multiply(n):
        gathers[n].e()
        out = sum(dot(xp[core], wg[n, core].reshape(1024, 512)) for core in range(2))
        for d in range(4):
            part = out[:, d * 128 : d * 128 + 128]
            own[n % 2, d] = part
            if n == 0:
                kvsend[d // 2, :, (d % 2) * 128 : (d % 2) * 128 + 128] = part.astype(BF)
            else:
                qsend[n - 1, d] = part.astype(BF)
        for cp in tiles(n):
            cp.start()

    def settle(n):
        for cp in tiles(n):
            cp.wait_recv()
        if n == 0:
            k = g // 2
            keys, value = own[0, 2 * k], own[0, 2 * k + 1]
            for d in range(3):
                keys = keys + kvrecv[d, :, :128].astype(F32)
                value = value + kvrecv[d, :, 128:].astype(F32)
            kv_ref[:, :128] = rotate(keys).astype(BF)
            kv_ref[:, 128:] = value.astype(BF)
            b_ref[...] = keys.astype(BF)
        else:
            query = own[n % 2, g]
            for d in range(3):
                query = query + qrecv[n - 1, d].astype(F32)
            ct_ref[n - 1] = query.astype(BF)
            rq_ref[n - 1] = (rotate(query) * (SCALE * LOG2E)).astype(BF)

    for step in range(CHUNKS + 4):
        for stage, n in (("d", step - 2), ("c", step - 1), ("b", step)):
            if 0 <= n < CHUNKS:
                getattr(gathers[n], stage)()
        if step + 2 < CHUNKS:
            gathers[step + 2].a()
        if 0 <= step - 2 < CHUNKS:
            multiply(step - 2)
        if 0 <= step - 3 < CHUNKS:
            settle(step - 3)
    total = rawsend[g]
    for d in range(3):
        raw_tile(d).wait_recv()
        total = total + rawrecv[d]
    raw_ref[...] = total
    for n in range(CHUNKS):
        gathers[n].sent()
        for cp in tiles(n):
            cp.wait_send()
    for d in range(3):
        raw_tile(d).wait_send()


def attend_kernel(
    rq_ref, ct_ref, kv_ref, b_ref, raw_ref, bias_ref, rate_ref, skip_ref,
    teacher_ref, student_ref,
    kvall, stall, acc, top, contrib, ssem, rsem,
):
    p = places()
    s = p["s"]
    kv = Gather(kvall, ssem.at[0], rsem.at[0], p, 256, True)
    st = Gather(stall, ssem.at[1], rsem.at[1], p, 256, True)
    kvall[p["c"], p["zy"]] = kv_ref[...]
    enter(["R", "L", "Z", "S"], p)
    kv.a()

    row = lax.broadcasted_iota(jnp.int32, (8, TOK), 0)

    def per_head(ref):
        out = jnp.full((8, TOK), ref[0], F32)
        for h in range(1, LOCAL_HEADS):
            out = jnp.where(row % LOCAL_HEADS == h, ref[h], out)
        return out

    arg = raw_ref[...] + per_head(bias_ref)
    step = jnp.maximum(arg, 0.0) + jnp.log1p(jnp.exp(-jnp.abs(arg)))
    decay = -per_head(rate_ref) * step
    from_t = lax.broadcasted_iota(jnp.int32, (STRETCH, STRETCH), 0)
    from_s = lax.broadcasted_iota(jnp.int32, (STRETCH, STRETCH), 1)
    causal = from_s <= from_t
    lower = causal.astype(F32)
    upper = (from_t <= from_s).astype(F32)
    pieces = []
    for i in range(2):
        part = decay[:, i * STRETCH : (i + 1) * STRETCH]
        cum_row = jnp.dot(part, upper, preferred_element_type=F32, precision=lax.Precision.HIGHEST)
        cum_col = dot_t(lower, part, lax.Precision.HIGHEST)
        pieces.append((cum_row, cum_col, step[:, i * STRETCH : (i + 1) * STRETCH]))
    values = [kv_ref[i * STRETCH : (i + 1) * STRETCH, 128:] for i in range(2)]
    bterm = [b_ref[i * STRETCH : (i + 1) * STRETCH] for i in range(2)]
    ends = [jnp.exp(jnp.broadcast_to(pieces[i][0][:, STRETCH - 1 :], (8, HEAD_DIM))) for i in range(2)]
    turned = [bterm[i].astype(F32).T for i in range(2)]
    for i in range(2):
        cum_row, _, rate = pieces[i]
        weight = jnp.exp(cum_row[:, STRETCH - 1 :] - cum_row) * rate
        for h in range(LOCAL_HEADS):
            contrib[i, h] = dot((turned[i] * weight[h : h + 1]).astype(BF), values[i])
    for h in range(LOCAL_HEADS):
        local = ends[1][h : h + 1] * contrib[0, h] + contrib[1, h]
        stall[p["c"], p["zy"], h * 128 : h * 128 + 128] = local.astype(BF)
    both = ends[0] * ends[1]
    high = both.astype(BF)
    low = (both - high.astype(F32)).astype(BF)
    stall[p["c"], p["zy"], 512:528] = jnp.concatenate([high, low], axis=0)
    st.a()
    kv.b()
    st.b()

    skips = [skip_ref[h] for h in range(LOCAL_HEADS)]
    for i in range(2):
        cum_row, cum_col, rate = pieces[i]
        rows = slice(i * STRETCH, (i + 1) * STRETCH)
        for h in range(LOCAL_HEADS):
            gram = dot_t(ct_ref[h, rows], bterm[i])
            diff = cum_col[:, h : h + 1] - cum_row[h : h + 1]
            mix = jnp.exp(jnp.where(causal, diff, FAR_BELOW)) * (rate[h : h + 1] * SCALE) * gram
            inside = dot(mix.astype(BF), values[i])
            acc[h, rows, :128] = inside + skips[h] * values[i].astype(F32)
    kv.c()
    st.c()
    kv.d()
    st.d()
    st.e()

    def advance(d, carried):
        block = stall.at[d % 2, d // 2]
        tail = block[512:528].astype(F32)
        total = tail[0:8] + tail[8:16]
        return tuple(
            total[h : h + 1] * carried[h] + block[h * 128 : h * 128 + 128].astype(F32)
            for h in range(LOCAL_HEADS)
        )

    zero = jnp.zeros((HEAD_DIM, HEAD_DIM), F32)
    incoming = lax.fori_loop(0, s, advance, (zero,) * LOCAL_HEADS)
    for i in range(2):
        _, cum_col, _ = pieces[i]
        rows = slice(i * STRETCH, (i + 1) * STRETCH)
        reach = jnp.exp(cum_col) * SCALE
        for h in range(LOCAL_HEADS):
            state = incoming[h] if i == 0 else ends[0][h : h + 1] * incoming[h] + contrib[0, h]
            carried = dot(ct_ref[h, rows], state.astype(BF))
            out = acc[h, rows, :128] + reach[:, h : h + 1] * carried
            student_ref[rows, h * 128 : h * 128 + 128] = out.astype(BF)

    kv.e()
    ones = jnp.ones((TOK, HEAD_DIM), BF)

    def absorb(keys, vals, masked, first):
        wide = jnp.concatenate([vals, ones], axis=1)
        for h in range(LOCAL_HEADS):
            for i in range(2):
                rows = slice(i * STRETCH, (i + 1) * STRETCH)
                scores = dot_t(rq_ref[h, rows], keys)
                if masked:
                    at_t = lax.broadcasted_iota(jnp.int32, scores.shape, 0) + i * STRETCH
                    at_u = lax.broadcasted_iota(jnp.int32, scores.shape, 1)
                    scores = jnp.where(at_u <= at_t, scores, FAR_BELOW)
                high = jnp.max(scores, axis=1, keepdims=True)
                if first:
                    now = jnp.broadcast_to(high, (STRETCH, 128))
                else:
                    now = jnp.maximum(top[h, rows], high)
                weights = jnp.exp2(scores - now[:, :1]).astype(BF)
                mixed = dot(weights, wide)
                if not first:
                    shrink = jnp.exp2(top[h, rows] - now)
                    mixed = mixed + acc[h, rows] * jnp.concatenate([shrink, shrink], axis=1)
                acc[h, rows] = mixed
                top[h, rows] = now

    absorb(kv_ref[:, :128], kv_ref[:, 128:], True, True)

    def visit(j, carry):
        block = kvall.at[j % 2, j // 2]
        absorb(block[:, :128], block[:, 128:], False, False)
        return carry

    lax.fori_loop(0, s, visit, 0)
    for h in range(LOCAL_HEADS):
        done = acc[h]
        teacher_ref[:, h * 128 : h * 128 + 128] = (done[:, :128] / done[:, 128:]).astype(BF)
    kv.sent()
    st.sent()


def tables():
    half = HEAD_DIM // 2
    freq = ROPE_BASE ** (-2.0 * np.arange(half) / HEAD_DIM)
    freq = np.concatenate([freq, freq])
    near = np.arange(TOK)[:, None] * freq[None]
    base = (np.arange(16) * TOK)[:, None] * freq[None]
    return (
        np.stack([np.cos(near), np.sin(near)]).astype(np.float32),
        np.stack([np.cos(base), np.sin(base)]).astype(np.float32),
    )


def body(layer_input, attn_weight, rate_weight, rate_bias, decay_rate, skip_gain):
    vmem = pl.BlockSpec(memory_space=pltpu.VMEM)
    smem = pl.BlockSpec(memory_space=pltpu.SMEM)
    dma = pltpu.SemaphoreType.DMA
    near, base = tables()
    heads = (LOCAL_HEADS, TOK, HEAD_DIM)
    rq, ct, kv, bterm, raw = pl.pallas_call(
        project_kernel,
        name="project",
        out_shape=(
            jax.ShapeDtypeStruct(heads, BF),
            jax.ShapeDtypeStruct(heads, BF),
            jax.ShapeDtypeStruct((TOK, 256), BF),
            jax.ShapeDtypeStruct((TOK, HEAD_DIM), BF),
            jax.ShapeDtypeStruct((8, TOK), F32),
        ),
        in_specs=[vmem] * 5,
        out_specs=(vmem,) * 5,
        scratch_shapes=[
            pltpu.VMEM((CHUNKS, 2, 8, 128, 512), BF),
            pltpu.VMEM((2, TOK, 1024), BF),
            pltpu.VMEM((2, 4, TOK, 128), F32),
            pltpu.VMEM((4, 4, TOK, 128), BF),
            pltpu.VMEM((4, 3, TOK, 128), BF),
            pltpu.VMEM((2, TOK, 256), BF),
            pltpu.VMEM((3, TOK, 256), BF),
            pltpu.VMEM((4, 8, TOK), F32),
            pltpu.VMEM((3, 8, TOK), F32),
            dma((CHUNKS, COPIES)),
            dma((CHUNKS, COPIES)),
            dma((CHUNKS + 1, 3)),
            dma((CHUNKS + 1, 3)),
        ],
        compiler_params=pltpu.CompilerParams(
            collective_id=0, has_side_effects=True, vmem_limit_bytes=56 * 2**20
        ),
    )(layer_input, attn_weight.reshape(128, 2560), rate_weight.T, jnp.asarray(near), jnp.asarray(base))
    return pl.pallas_call(
        attend_kernel,
        name="attend",
        out_shape=(
            jax.ShapeDtypeStruct((TOK, 512), BF),
            jax.ShapeDtypeStruct((TOK, 512), BF),
        ),
        in_specs=[vmem] * 5 + [smem] * 3,
        out_specs=(vmem, vmem),
        scratch_shapes=[
            pltpu.VMEM((2, 8, TOK, 256), BF),
            pltpu.VMEM((2, 8, 528, 128), BF),
            pltpu.VMEM((LOCAL_HEADS, TOK, 256), F32),
            pltpu.VMEM((LOCAL_HEADS, TOK, 128), F32),
            pltpu.VMEM((2, LOCAL_HEADS, HEAD_DIM, HEAD_DIM), F32),
            dma((2, COPIES)),
            dma((2, COPIES)),
        ],
        compiler_params=pltpu.CompilerParams(
            collective_id=1, has_side_effects=True, vmem_limit_bytes=56 * 2**20
        ),
    )(rq, ct, kv, bterm, raw, rate_bias, decay_rate, skip_gain)


def solution(mesh):
    placed = (
        P("seq", "grp"),
        P(("grp", "seq"), "mdl", None),
        P("grp", "mdl"),
        P(("mdl", "grp")),
        P(("mdl", "grp")),
        P(("mdl", "grp")),
    )
    return jax.shard_map(
        body,
        mesh=mesh,
        in_specs=placed,
        out_specs=(P("seq", ("mdl", "grp")), P("seq", ("mdl", "grp"))),
        check_vma=False,
    )
```

```python
import functools
import math

import jax
import jax.numpy as jnp
import numpy as np
from jax import lax
from jax.experimental import pallas as pl
from jax.experimental.pallas import tpu as pltpu
from jax.sharding import PartitionSpec as P

HEAD_DIM = 128
STRETCH = 256
ROPE_BASE = 500000.0
FAR_BELOW = -1e30
TOK = 512
LOCAL_HEADS = 4
CHUNKS = 5
COPIES = 11
HALF = 256
SCALE = HEAD_DIM**-0.5
LOG2E = math.log2(math.e)
MESH = pl.DeviceIdType.MESH
BF = jnp.bfloat16
F32 = jnp.float32


def places():
    g, s, m = lax.axis_index("grp"), lax.axis_index("seq"), lax.axis_index("mdl")
    zh, y, c = s // 8, (s // 2) % 4, s % 2

    def seq(zh, y, c):
        return zh * 8 + y * 2 + c

    up, down, far = lax.rem(y + 1, 4), lax.rem(y + 3, 4), lax.rem(y + 2, 4)
    return {
        "g": g, "s": s, "zh": zh, "y": y, "c": c,
        "zy": zh * 4 + y,
        "up": up, "down": down, "far": far,
        "R": (g, seq(zh, up, c), m),
        "L": (g, seq(zh, down, c), m),
        "Z": (g, seq(1 - zh, y, c), m),
        "S": (g, seq(zh, y, 1 - c), m),
        "G": [(lax.rem(g + d, 4), s, m) for d in (1, 2, 3)],
    }


def enter(names, p):
    bar = pltpu.get_barrier_semaphore()
    targets = []
    for name in names:
        targets += p[name] if name == "G" else [p[name]]
    for dev in targets:
        pl.semaphore_signal(bar, inc=1, device_id=dev, device_id_type=MESH)
    pl.semaphore_wait(bar, len(targets))


class Gather:
    def __init__(self, buf, ssem, rsem, p, half):
        self.buf, self.ssem, self.rsem, self.p = buf, ssem, rsem, p
        self.rows, self.half = buf.shape[-2], half

    def remote(self, k, ref, dev):
        return pltpu.make_async_remote_copy(
            src_ref=ref, dst_ref=ref, send_sem=self.ssem.at[k], recv_sem=self.rsem.at[k],
            device_id=dev, device_id_type=MESH,
        )

    def copy(self, k, dev, zy, first=None, count=None):
        c = self.p["c"]
        ref = self.buf.at[c, zy] if first is None else self.buf.at[c, zy, pl.ds(first, count)]
        return self.remote(k, ref, dev)

    def four(self, k, own, core):
        return self.remote(k, self.buf.at[core, pl.ds(self.base(own), 4)], self.p["S"])

    def base(self, own):
        return (self.p["zh"] if own else 1 - self.p["zh"]) * 4

    def spread(self, own):
        p, k = self.p, 0 if own else 5
        at = self.base(own) + p["y"]
        return self.copy(k, p["R"], at), self.copy(k + 1, p["L"], at)

    def arrive(self, own):
        p, k = self.p, 0 if own else 5
        return (
            self.copy(k, p["R"], self.base(own) + p["down"]),
            self.copy(k + 1, p["L"], self.base(own) + p["up"]),
        )

    def pair(self, own, left, right):
        p, k = self.p, 2 if own else 7
        return (
            self.copy(k, p["R"], self.base(own) + left, 0, self.half),
            self.copy(k + 1, p["L"], self.base(own) + right, self.half, self.rows - self.half),
        )

    def forward(self, own):
        return self.pair(own, self.p["down"], self.p["up"])

    def halves(self, own):
        return self.pair(own, self.p["far"], self.p["far"])

    def across(self, own):
        return self.copy(4, self.p["Z"], self.base(own) + self.p["y"])

    def a(self):
        for cp in self.spread(True):
            cp.start()
        self.across(True).start()

    def pass_on(self, own):
        for got, on in zip(self.arrive(own), self.forward(own)):
            got.wait_recv()
            on.start()

    def b(self):
        self.pass_on(True)
        self.across(False).wait_recv()
        for cp in self.spread(False):
            cp.start()

    def finish(self, own):
        for cp in self.halves(own):
            cp.wait_recv()
        self.four(9 if own else 10, own, self.p["c"]).start()

    def c(self):
        self.finish(True)
        self.pass_on(False)

    def d(self):
        self.finish(False)

    def e(self):
        for own in (True, False):
            self.four(9 if own else 10, own, 1 - self.p["c"]).wait_recv()

    def sent(self):
        for own in (True, False):
            for cp in (*self.spread(own), *self.forward(own)):
                cp.wait_send()
            self.four(9 if own else 10, own, self.p["c"]).wait_send()
        self.across(True).wait_send()


class Earlier(Gather):
    def lift(self, n):
        at = [self.p["y"], self.p["down"], self.p["up"], self.p["far"]][n]
        return self.copy(4 + n, self.p["Z"], at)

    def low(self, f):
        pl.when(self.p["zh"] == 0)(f)

    def high(self, f):
        pl.when(self.p["zh"] == 1)(f)

    def a(self):
        for cp in self.spread(True):
            cp.start()
        self.low(lambda: self.lift(0).start())

    def b(self):
        self.pass_on(True)

        def send():
            self.lift(1).start()
            self.lift(2).start()

        self.low(send)

    def c(self):
        self.finish(True)
        self.low(lambda: self.lift(3).start())

    def near(self):
        self.four(9, True, 1 - self.p["c"]).wait_recv()

    def d(self):
        def hand():
            for n in range(4):
                self.lift(n).wait_recv()
            self.four(10, False, self.p["c"]).start()

        self.high(hand)

    def e(self):
        self.high(lambda: self.four(10, False, 1 - self.p["c"]).wait_recv())

    def sent(self):
        for cp in (*self.spread(True), *self.forward(True)):
            cp.wait_send()
        self.four(9, True, self.p["c"]).wait_send()

        def lifted():
            for n in range(4):
                self.lift(n).wait_send()

        self.low(lifted)
        self.high(lambda: self.four(10, False, self.p["c"]).wait_send())


def dot(a, b):
    return jnp.dot(a, b, preferred_element_type=F32)


def dot_t(a, b, precision=None):
    return lax.dot_general(
        a, b, (((1,), (1,)), ((), ())), preferred_element_type=F32, precision=precision
    )


def window_kernel(
    x_ref, w_ref, rate_w_ref, near_ref, base_ref, bias_ref, rate_ref, skip_ref,
    teacher_ref, student_ref,
    wg, xp, own, qsend, qrecv, kvsend, kvrecv, rawsend, rawrecv,
    kvall, stall, sx, rq, ct, vrow, brow, contrib, inner, acc, top,
    wssem, wrsem, gssem, grsem, kssem, krsem, xssem, xrsem,
):
    p = places()
    g, s, zh, c, zy = p["g"], p["s"], p["zh"], p["c"], p["zy"]
    gathers = [Gather(wg.at[n], wssem.at[n], wrsem.at[n], p, 64) for n in range(CHUNKS)]
    kv = Earlier(kvall, kssem.at[0], krsem.at[0], p, 128)
    st = Earlier(stall, kssem.at[1], krsem.at[1], p, 128)

    def place(chunk):
        for d in range(4):
            k = d // 2
            first = k * 1280 + (1024 + (d % 2) * 128 if chunk == 0 else (d % 2) * 512 + (chunk - 1) * 128)
            wg[chunk, c, zy, :, d * 128 : d * 128 + 128] = w_ref[:, first : first + 128]

    def tile(source, target, k, d):
        return pltpu.make_async_remote_copy(
            src_ref=source, dst_ref=target, send_sem=gssem.at[k, d], recv_sem=grsem.at[k, d],
            device_id=p["G"][d], device_id_type=MESH,
        )

    def raw_tile(d):
        return tile(rawsend.at[lax.rem(g + d + 1, 4)], rawrecv.at[d], CHUNKS, d)

    def tiles(n):
        if n == 0:
            return [tile(kvsend.at[lax.rem(g + d + 1, 4) // 2], kvrecv.at[d], 0, d) for d in range(3)]
        return [tile(qsend.at[n - 1, lax.rem(g + d + 1, 4)], qrecv.at[n - 1, d], n, d) for d in range(3)]

    def rotate(u):
        near_c, near_s = near_ref[0], near_ref[1]
        far_c, far_s = base_ref[0, pl.ds(s, 1), :], base_ref[1, pl.ds(s, 1), :]
        lane = lax.broadcasted_iota(jnp.int32, (1, HEAD_DIM), 1)
        sign = jnp.where(lane < HEAD_DIM // 2, -1.0, 1.0)
        cosine = near_c * far_c - near_s * far_s
        sine = (near_s * far_c + near_c * far_s) * sign
        return u * cosine + pltpu.roll(u, HEAD_DIM // 2, 1) * sine

    def multiply(n):
        gathers[n].e()
        out = sum(dot(xp[core], wg[n, core].reshape(1024, 512)) for core in range(2))
        for d in range(4):
            part = out[:, d * 128 : d * 128 + 128]
            own[n % 2, d] = part
            if n == 0:
                kvsend[d // 2, :, (d % 2) * 128 : (d % 2) * 128 + 128] = part.astype(BF)
            else:
                qsend[n - 1, d] = part.astype(BF)
        for cp in tiles(n):
            cp.start()

    def settle(n):
        for cp in tiles(n):
            cp.wait_recv()
        if n == 0:
            k = g // 2
            keys, value = own[0, 2 * k], own[0, 2 * k + 1]
            for d in range(3):
                keys = keys + kvrecv[d, :, :128].astype(F32)
                value = value + kvrecv[d, :, 128:].astype(F32)
            turned = rotate(keys).astype(BF)
            for i in range(4):
                kvall[c, zy, :128, i * 128 : i * 128 + 128] = turned[i * 128 : i * 128 + 128]
            kvall[c, zy, 128:] = value.T.astype(BF)
            vrow[...] = value.astype(BF)
            brow[...] = keys.astype(BF)
        else:
            query = own[n % 2, g]
            for d in range(3):
                query = query + qrecv[n - 1, d].astype(F32)
            ct[n - 1] = query.astype(BF)
            rq[n - 1] = (rotate(query) * (SCALE * LOG2E)).astype(BF)

    row = lax.broadcasted_iota(jnp.int32, (8, TOK), 0)

    def per_head(ref):
        out = jnp.full((8, TOK), ref[0], F32)
        for h in range(1, LOCAL_HEADS):
            out = jnp.where(row % LOCAL_HEADS == h, ref[h], out)
        return out

    from_t = lax.broadcasted_iota(jnp.int32, (STRETCH, STRETCH), 0)
    from_s = lax.broadcasted_iota(jnp.int32, (STRETCH, STRETCH), 1)
    causal = from_s <= from_t
    rows_of = [slice(i * STRETCH, (i + 1) * STRETCH) for i in range(2)]

    def decays():
        total = rawsend[g]
        for d in range(3):
            raw_tile(d).wait_recv()
            total = total + rawrecv[d]
        arg = total + per_head(bias_ref)
        step = jnp.maximum(arg, 0.0) + jnp.log1p(jnp.exp(-jnp.abs(arg)))
        decay = -per_head(rate_ref) * step
        lower = causal.astype(F32)
        upper = (from_t <= from_s).astype(F32)
        pieces = []
        for i in range(2):
            part = decay[:, rows_of[i]]
            cum_row = jnp.dot(part, upper, preferred_element_type=F32, precision=lax.Precision.HIGHEST)
            cum_col = dot_t(lower, part, lax.Precision.HIGHEST)
            end = jnp.exp(jnp.broadcast_to(cum_row[:, STRETCH - 1 :], (8, HEAD_DIM)))
            pieces.append((cum_row, cum_col, step[:, rows_of[i]], end))
        return pieces

    def swap():
        return pltpu.make_async_remote_copy(
            src_ref=sx.at[c], dst_ref=sx.at[c], send_sem=xssem, recv_sem=xrsem,
            device_id=p["S"], device_id_type=MESH,
        )

    def swapped():
        return pltpu.make_async_remote_copy(
            src_ref=sx.at[1 - c], dst_ref=sx.at[1 - c], send_sem=xssem, recv_sem=xrsem,
            device_id=p["S"], device_id_type=MESH,
        )

    def split(value):
        high = value.astype(BF)
        return jnp.concatenate([high, (value - high.astype(F32)).astype(BF)], axis=0)

    def local_state(pieces):
        for i in range(2):
            cum_row, _, rate, _ = pieces[i]
            turned = brow[rows_of[i]].astype(F32).T
            weight = jnp.exp(cum_row[:, STRETCH - 1 :] - cum_row) * rate
            for h in range(LOCAL_HEADS):
                contrib[i, h] = dot((turned * weight[h : h + 1]).astype(BF), vrow[rows_of[i]])
        for h in range(LOCAL_HEADS):
            local = pieces[1][3][h : h + 1] * contrib[0, h] + contrib[1, h]
            sx[c, h * 128 : h * 128 + 128] = local.astype(BF)
        sx[c, 512:528] = split(pieces[0][3] * pieces[1][3])
        swap().start()

    def whole(ref, first):
        both = ref[first : first + 16].astype(F32)
        return both[:8] + both[8:]

    def chip_state():
        swapped().wait_recv()
        first, second = whole(sx.at[0], 512), whole(sx.at[1], 512)
        for k in range(2):
            at = pl.ds(pl.multiple_of(c * 256 + k * 128, 128), 128)
            decay = jnp.where(c == 0, second[k : k + 1], second[k + 2 : k + 3])
            both = decay * sx[0, at].astype(F32) + sx[1, at].astype(F32)
            stall[c, zy, k * 128 : k * 128 + 128] = both.astype(BF)
        stall[c, zy, 256:272] = split(first * second)

    def inside(pieces, h):
        for i in range(2):
            cum_row, cum_col, rate, _ = pieces[i]
            gram = dot_t(ct[h, rows_of[i]], brow[rows_of[i]])
            diff = cum_col[:, h : h + 1] - cum_row[h : h + 1]
            mix = jnp.exp(jnp.where(causal, diff, FAR_BELOW)) * (rate[h : h + 1] * SCALE) * gram
            value = vrow[rows_of[i]]
            inner[h, rows_of[i]] = dot(mix.astype(BF), value) + skip_ref[h] * value.astype(F32)

    def arriving():
        def advance(d, carried):
            blocks = [stall.at[k, d] for k in range(2)]
            total = whole(blocks[0], 256)
            return tuple(
                total[h : h + 1] * carried[h]
                + blocks[h // 2][h % 2 * 128 : h % 2 * 128 + 128].astype(F32)
                for h in range(LOCAL_HEADS)
            )

        zero = jnp.zeros((HEAD_DIM, HEAD_DIM), F32)
        carried = lax.fori_loop(0, zy, advance, (zero,) * LOCAL_HEADS)
        first = whole(sx.at[0], 512)
        return [
            jnp.where(
                c == 0, carried[h],
                first[h : h + 1] * carried[h] + sx[0, h * 128 : h * 128 + 128].astype(F32),
            )
            for h in range(LOCAL_HEADS)
        ]

    def student(pieces, incoming, h):
        for i in range(2):
            reach = jnp.exp(pieces[i][1]) * SCALE
            state = incoming[h] if i == 0 else pieces[0][3][h : h + 1] * incoming[h] + contrib[0, h]
            carried = dot(ct[h, rows_of[i]], state.astype(BF))
            out = inner[h, rows_of[i]] + reach[:, h : h + 1] * carried
            student_ref[rows_of[i], h * 128 : h * 128 + 128] = out.astype(BF)

    ones = jnp.ones((16, TOK), BF)

    def absorb(blocks, heads, diagonal=False):
        todo = [(b, h, i) for b in range(len(blocks)) for h in heads for i in range(TOK // HALF)]

        def scores(n):
            b, h, i = todo[n]
            keys = jnp.concatenate([blocks[b][:128, k * 128 : k * 128 + 128] for k in range(4)], axis=0)
            out = dot_t(keys, rq[h, i * HALF : i * HALF + HALF])
            if diagonal:
                at_u = lax.broadcasted_iota(jnp.int32, out.shape, 0)
                at_t = lax.broadcasted_iota(jnp.int32, out.shape, 1) + i * HALF
                out = jnp.where(at_u <= at_t, out, FAR_BELOW)
            return out

        found = {n: scores(n) for n in range(min(2, len(todo)))}
        ready = None
        for n in range(len(todo) + 1):
            now = None
            if n + 2 < len(todo):
                found[n + 2] = scores(n + 2)
            if n < len(todo):
                b, h, i = todo[n]
                cols = slice(i * HALF, i * HALF + HALF)
                score = found.pop(n)
                high = jnp.max(score, axis=0, keepdims=True)
                if diagonal:
                    peak, shrink = high, None
                else:
                    before = top[h, 0:1, cols]
                    peak = jnp.maximum(before, high)
                    shrink = jnp.exp2(before - peak)
                now = (b, h, cols, jnp.exp2(score - peak).astype(BF), shrink)
                top[h, 0:1, cols] = peak
            if ready is not None:
                b, h, cols, weights, shrink = ready
                mixed = dot(jnp.concatenate([blocks[b][128:], ones], axis=0), weights)
                acc[h, :, cols] = mixed if diagonal else mixed + acc[h, :, cols] * shrink
            ready = now

    def own_part(heads):
        absorb([kvall.at[c, zy]], heads, True)

        def visit(j, carry):
            absorb([kvall.at[j % 2, j // 2]], heads)
            return carry

        lax.fori_loop(zh * 8, s, visit, 0)

    def low_part(heads):
        def visit(j, carry):
            absorb([kvall.at[0, j], kvall.at[1, j]], heads)
            return carry

        lax.fori_loop(0, zh * 4, visit, 0)

    def teacher(h):
        done = acc[h]
        out = (done[:128] / done[128:129]).T
        teacher_ref[:, h * 128 : h * 128 + 128] = out.astype(BF)

    w = gathers
    place(0)
    enter(["R", "L", "Z", "S", "G"], p)
    w[0].a()
    place(1)
    w[1].a()
    place(2)
    w[2].a()
    raw = dot_t(rate_w_ref[...], x_ref[...])
    for d in range(4):
        rawsend[d] = jnp.concatenate([raw[4 * d : 4 * d + 4], raw[4 * d : 4 * d + 4]], axis=0)
    for d in range(3):
        raw_tile(d).start()
    place(3)
    place(4)
    for core in range(2):
        for at in range(8):
            src = (at * 2 + core) * 128
            xp[core, :, at * 128 : at * 128 + 128] = x_ref[:, src : src + 128]
    pieces = decays()
    w[0].b()
    w[3].a()
    w[1].b()
    w[0].c()
    w[0].d()
    multiply(0)
    w[4].a()
    w[1].c()
    w[2].b()
    settle(0)
    kv.a()
    w[1].d()
    multiply(1)
    local_state(pieces)
    w[2].c()
    w[3].b()
    kv.b()
    chip_state()
    st.a()
    settle(1)
    inside(pieces, 0)
    w[2].d()
    multiply(2)
    kv.c()
    st.b()
    w[3].c()
    w[4].b()
    settle(2)
    inside(pieces, 1)
    st.c()
    kv.near()
    own_part([0])
    w[3].d()
    multiply(3)
    w[4].c()
    own_part([1])
    settle(3)
    inside(pieces, 2)
    w[4].d()
    st.d()
    st.near()
    own_part([2])
    multiply(4)
    kv.d()
    st.e()
    incoming = arriving()
    for h in range(3):
        student(pieces, incoming, h)
    kv.e()
    low_part([0])
    low_part([1])
    settle(4)
    inside(pieces, 3)
    student(pieces, incoming, 3)
    low_part([2])
    own_part([3])
    low_part([3])
    for h in range(LOCAL_HEADS):
        teacher(h)
    for n in range(CHUNKS):
        w[n].sent()
        for cp in tiles(n):
            cp.wait_send()
    for d in range(3):
        raw_tile(d).wait_send()
    kv.sent()
    st.sent()
    swap().wait_send()


def tables():
    half = HEAD_DIM // 2
    freq = ROPE_BASE ** (-2.0 * np.arange(half) / HEAD_DIM)
    freq = np.concatenate([freq, freq])
    near = np.arange(TOK)[:, None] * freq[None]
    base = (np.arange(16) * TOK)[:, None] * freq[None]
    return (
        np.stack([np.cos(near), np.sin(near)]).astype(np.float32),
        np.stack([np.cos(base), np.sin(base)]).astype(np.float32),
    )


def body(layer_input, attn_weight, rate_weight, rate_bias, decay_rate, skip_gain):
    vmem = pl.BlockSpec(memory_space=pltpu.VMEM)
    smem = pl.BlockSpec(memory_space=pltpu.SMEM)
    dma = pltpu.SemaphoreType.DMA
    near, base = tables()
    heads = (LOCAL_HEADS, TOK, HEAD_DIM)
    return pl.pallas_call(
        window_kernel,
        name="window",
        out_shape=(
            jax.ShapeDtypeStruct((TOK, 512), BF),
            jax.ShapeDtypeStruct((TOK, 512), BF),
        ),
        in_specs=[vmem] * 5 + [smem] * 3,
        out_specs=(vmem, vmem),
        scratch_shapes=[
            pltpu.VMEM((CHUNKS, 2, 8, 128, 512), BF),
            pltpu.VMEM((2, TOK, 1024), BF),
            pltpu.VMEM((2, 4, TOK, 128), F32),
            pltpu.VMEM((4, 4, TOK, 128), BF),
            pltpu.VMEM((4, 3, TOK, 128), BF),
            pltpu.VMEM((2, TOK, 256), BF),
            pltpu.VMEM((3, TOK, 256), BF),
            pltpu.VMEM((4, 8, TOK), F32),
            pltpu.VMEM((3, 8, TOK), F32),
            pltpu.VMEM((2, 8, 256, TOK), BF),
            pltpu.VMEM((2, 8, 272, 128), BF),
            pltpu.VMEM((2, 528, 128), BF),
            pltpu.VMEM(heads, BF),
            pltpu.VMEM(heads, BF),
            pltpu.VMEM((TOK, HEAD_DIM), BF),
            pltpu.VMEM((TOK, HEAD_DIM), BF),
            pltpu.VMEM((2, LOCAL_HEADS, HEAD_DIM, HEAD_DIM), F32),
            pltpu.VMEM(heads, F32),
            pltpu.VMEM((LOCAL_HEADS, 144, TOK), F32),
            pltpu.VMEM((LOCAL_HEADS, 8, TOK), F32),
            dma((CHUNKS, COPIES)),
            dma((CHUNKS, COPIES)),
            dma((CHUNKS + 1, 3)),
            dma((CHUNKS + 1, 3)),
            dma((2, COPIES)),
            dma((2, COPIES)),
            dma,
            dma,
        ],
        compiler_params=pltpu.CompilerParams(
            collective_id=0, has_side_effects=True, vmem_limit_bytes=58 * 2**20
        ),
    )(
        layer_input, attn_weight.reshape(128, 2560), rate_weight.T, jnp.asarray(near),
        jnp.asarray(base), rate_bias, decay_rate, skip_gain,
    )


def solution(mesh):
    placed = (
        P("seq", "grp"),
        P(("grp", "seq"), "mdl", None),
        P("grp", "mdl"),
        P(("mdl", "grp")),
        P(("mdl", "grp")),
        P(("mdl", "grp")),
    )
    return jax.shard_map(
        body,
        mesh=mesh,
        in_specs=placed,
        out_specs=(P("seq", ("mdl", "grp")), P("seq", ("mdl", "grp"))),
        check_vma=False,
    )
```

```python
import functools
import math

import jax
import jax.numpy as jnp
import numpy as np
from jax import lax
from jax.experimental import pallas as pl
from jax.experimental.pallas import tpu as pltpu
from jax.sharding import PartitionSpec as P

HEAD_DIM = 128
STRETCH = 256
ROPE_BASE = 500000.0
FAR_BELOW = -1e30
TOK = 512
LOCAL_HEADS = 4
KINDS = ("k", "v", "q0", "q1", "q2", "q3")
COPIES = 11
HALF = 256
SCALE = HEAD_DIM**-0.5
LOG2E = math.log2(math.e)
MESH = pl.DeviceIdType.MESH
BF = jnp.bfloat16
F32 = jnp.float32


def places():
    g, s, m = lax.axis_index("grp"), lax.axis_index("seq"), lax.axis_index("mdl")
    zh, y, c = s // 8, (s // 2) % 4, s % 2

    def seq(zh, y, c):
        return zh * 8 + y * 2 + c

    up, down, far = lax.rem(y + 1, 4), lax.rem(y + 3, 4), lax.rem(y + 2, 4)
    return {
        "g": g, "s": s, "zh": zh, "y": y, "c": c,
        "zy": zh * 4 + y,
        "up": up, "down": down, "far": far,
        "R": (g, seq(zh, up, c), m),
        "L": (g, seq(zh, down, c), m),
        "Z": (g, seq(1 - zh, y, c), m),
        "S": (g, seq(zh, y, 1 - c), m),
        "G": [(lax.rem(g + d, 4), s, m) for d in (1, 2, 3)],
    }


def enter(names, p):
    bar = pltpu.get_barrier_semaphore()
    targets = []
    for name in names:
        targets += p[name] if name == "G" else [p[name]]
    for dev in targets:
        pl.semaphore_signal(bar, inc=1, device_id=dev, device_id_type=MESH)
    pl.semaphore_wait(bar, len(targets))


class Gather:
    def __init__(self, buf, ssem, rsem, p, half):
        self.buf, self.ssem, self.rsem, self.p = buf, ssem, rsem, p
        self.rows, self.half = buf.shape[-2], half

    def remote(self, k, ref, dev):
        return pltpu.make_async_remote_copy(
            src_ref=ref, dst_ref=ref, send_sem=self.ssem.at[k], recv_sem=self.rsem.at[k],
            device_id=dev, device_id_type=MESH,
        )

    def copy(self, k, dev, zy, first=None, count=None):
        c = self.p["c"]
        ref = self.buf.at[c, zy] if first is None else self.buf.at[c, zy, pl.ds(first, count)]
        return self.remote(k, ref, dev)

    def four(self, k, own, core):
        return self.remote(k, self.buf.at[core, pl.ds(self.base(own), 4)], self.p["S"])

    def base(self, own):
        return (self.p["zh"] if own else 1 - self.p["zh"]) * 4

    def spread(self, own):
        p, k = self.p, 0 if own else 5
        at = self.base(own) + p["y"]
        return self.copy(k, p["R"], at), self.copy(k + 1, p["L"], at)

    def arrive(self, own):
        p, k = self.p, 0 if own else 5
        return (
            self.copy(k, p["R"], self.base(own) + p["down"]),
            self.copy(k + 1, p["L"], self.base(own) + p["up"]),
        )

    def pair(self, own, left, right):
        p, k = self.p, 2 if own else 7
        return (
            self.copy(k, p["R"], self.base(own) + left, 0, self.half),
            self.copy(k + 1, p["L"], self.base(own) + right, self.half, self.rows - self.half),
        )

    def forward(self, own):
        return self.pair(own, self.p["down"], self.p["up"])

    def halves(self, own):
        return self.pair(own, self.p["far"], self.p["far"])

    def across(self, own):
        return self.copy(4, self.p["Z"], self.base(own) + self.p["y"])

    def ay(self):
        for cp in self.spread(True):
            cp.start()

    def az(self):
        self.across(True).start()

    def pass_on(self, own):
        for got, on in zip(self.arrive(own), self.forward(own)):
            got.wait_recv()
            on.start()

    def f(self):
        self.pass_on(True)

    def zs(self):
        self.across(False).wait_recv()
        for cp in self.spread(False):
            cp.start()

    def finish(self, own):
        for cp in self.halves(own):
            cp.wait_recv()
        self.four(9 if own else 10, own, self.p["c"]).start()

    def s1(self):
        self.finish(True)

    def zf(self):
        self.pass_on(False)

    def s2(self):
        self.finish(False)

    def e(self):
        for own in (True, False):
            self.four(9 if own else 10, own, 1 - self.p["c"]).wait_recv()

    def sent(self):
        for own in (True, False):
            for cp in (*self.spread(own), *self.forward(own)):
                cp.wait_send()
            self.four(9 if own else 10, own, self.p["c"]).wait_send()
        self.across(True).wait_send()


class Earlier(Gather):
    def lift(self, n):
        at = [self.p["y"], self.p["down"], self.p["up"], self.p["far"]][n]
        return self.copy(4 + n, self.p["Z"], at)

    def low(self, f):
        pl.when(self.p["zh"] == 0)(f)

    def high(self, f):
        pl.when(self.p["zh"] == 1)(f)

    def a(self):
        for cp in self.spread(True):
            cp.start()
        self.low(lambda: self.lift(0).start())

    def b(self):
        self.pass_on(True)

        def send():
            self.lift(1).start()
            self.lift(2).start()

        self.low(send)

    def c(self):
        self.finish(True)
        self.low(lambda: self.lift(3).start())

    def near(self):
        self.four(9, True, 1 - self.p["c"]).wait_recv()

    def d(self):
        def hand():
            for n in range(4):
                self.lift(n).wait_recv()
            self.four(10, False, self.p["c"]).start()

        self.high(hand)

    def e(self):
        self.high(lambda: self.four(10, False, 1 - self.p["c"]).wait_recv())

    def sent(self):
        for cp in (*self.spread(True), *self.forward(True)):
            cp.wait_send()
        self.four(9, True, self.p["c"]).wait_send()

        def lifted():
            for n in range(4):
                self.lift(n).wait_send()

        self.low(lifted)
        self.high(lambda: self.four(10, False, self.p["c"]).wait_send())


def dot(a, b):
    return jnp.dot(a, b, preferred_element_type=F32)


def dot_t(a, b, precision=None):
    return lax.dot_general(
        a, b, (((1,), (1,)), ((), ())), preferred_element_type=F32, precision=precision
    )


def window_kernel(
    x_ref, w_ref, rate_w_ref, near_ref, base_ref, bias_ref, rate_ref, skip_ref,
    teacher_ref, student_ref,
    wkv, wq, xp, own_kv, own_q, qsend, qrecv, kvsend, kvrecv, rawsend, rawrecv,
    kall, vall, stall, sx, rq, ct, vrow, brow, contrib, inner, acc, top,
    wssem, wrsem, gssem, grsem, kssem, krsem, xssem, xrsem,
):
    p = places()
    g, s, zh, c, zy = p["g"], p["s"], p["zh"], p["c"], p["zy"]
    w = {}
    for n, name in enumerate(KINDS):
        buf = wkv.at[n] if n < 2 else wq.at[n - 2]
        w[name] = Gather(buf, wssem.at[n], wrsem.at[n], p, 64)
    kept = {
        name: Earlier(buf, kssem.at[n], krsem.at[n], p, half)
        for n, (name, buf, half) in enumerate((("k", kall, 64), ("v", vall, 64), ("s", stall, 128)))
    }

    def place(name):
        if name in "kv":
            n = "kv".index(name)
            for k in range(2):
                first = k * 1280 + 1024 + n * 128
                wkv[n, c, zy, :, k * 128 : k * 128 + 128] = w_ref[:, first : first + 128]
            return
        n = int(name[1])
        for d in range(4):
            first = d // 2 * 1280 + d % 2 * 512 + n * 128
            wq[n, c, zy, :, d * 128 : d * 128 + 128] = w_ref[:, first : first + 128]

    def tile(source, target, k, d):
        return pltpu.make_async_remote_copy(
            src_ref=source, dst_ref=target, send_sem=gssem.at[k, d], recv_sem=grsem.at[k, d],
            device_id=p["G"][d], device_id_type=MESH,
        )

    def raw_tile(d):
        return tile(rawsend.at[lax.rem(g + d + 1, 4)], rawrecv.at[d], len(KINDS), d)

    def tiles(name):
        k = KINDS.index(name)
        if k < 2:
            return [
                tile(kvsend.at[k, lax.rem(g + d + 1, 4) // 2], kvrecv.at[k, d], k, d) for d in range(3)
            ]
        return [
            tile(qsend.at[k - 2, lax.rem(g + d + 1, 4)], qrecv.at[k - 2, d], k, d) for d in range(3)
        ]

    def send_raw():
        raw = dot_t(rate_w_ref[...], x_ref[...])
        for d in range(4):
            rawsend[d] = jnp.concatenate([raw[4 * d : 4 * d + 4], raw[4 * d : 4 * d + 4]], axis=0)
        for d in range(3):
            raw_tile(d).start()

    def arrange():
        for core in range(2):
            for at in range(8):
                src = (at * 2 + core) * 128
                xp[core, :, at * 128 : at * 128 + 128] = x_ref[:, src : src + 128]

    def rotate(u):
        near_c, near_s = near_ref[0], near_ref[1]
        far_c, far_s = base_ref[0, pl.ds(s, 1), :], base_ref[1, pl.ds(s, 1), :]
        lane = lax.broadcasted_iota(jnp.int32, (1, HEAD_DIM), 1)
        sign = jnp.where(lane < HEAD_DIM // 2, -1.0, 1.0)
        cosine = near_c * far_c - near_s * far_s
        sine = (near_s * far_c + near_c * far_s) * sign
        return u * cosine + pltpu.roll(u, HEAD_DIM // 2, 1) * sine

    def multiply(name):
        w[name].e()
        k = KINDS.index(name)
        buf = wkv.at[k] if k < 2 else wq.at[k - 2]
        out = sum(dot(xp[core], buf[core].reshape(1024, buf.shape[-1])) for core in range(2))
        for d in range(buf.shape[-1] // 128):
            part = out[:, d * 128 : d * 128 + 128]
            if k < 2:
                own_kv[k, d] = part
                kvsend[k, d] = part.astype(BF)
            else:
                own_q[k % 2, d] = part
                qsend[k - 2, d] = part.astype(BF)
        for cp in tiles(name):
            cp.start()

    def settle(name):
        k = KINDS.index(name)
        for cp in tiles(name):
            cp.wait_recv()
        got = own_kv[k, g // 2] if k < 2 else own_q[k % 2, g]
        for d in range(3):
            got = got + (kvrecv[k, d] if k < 2 else qrecv[k - 2, d]).astype(F32)
        if name == "k":
            turned = rotate(got).astype(BF)
            for i in range(4):
                kall[c, zy, :, i * 128 : i * 128 + 128] = turned[i * 128 : i * 128 + 128]
            brow[...] = got.astype(BF)
        elif name == "v":
            vall[c, zy] = got.T.astype(BF)
            vrow[...] = got.astype(BF)
        else:
            ct[k - 2] = got.astype(BF)
            rq[k - 2] = (rotate(got) * (SCALE * LOG2E)).astype(BF)

    row = lax.broadcasted_iota(jnp.int32, (8, TOK), 0)

    def per_head(ref):
        out = jnp.full((8, TOK), ref[0], F32)
        for h in range(1, LOCAL_HEADS):
            out = jnp.where(row % LOCAL_HEADS == h, ref[h], out)
        return out

    from_t = lax.broadcasted_iota(jnp.int32, (STRETCH, STRETCH), 0)
    from_s = lax.broadcasted_iota(jnp.int32, (STRETCH, STRETCH), 1)
    causal = from_s <= from_t
    rows_of = [slice(i * STRETCH, (i + 1) * STRETCH) for i in range(2)]

    def decays():
        total = rawsend[g]
        for d in range(3):
            raw_tile(d).wait_recv()
            total = total + rawrecv[d]
        arg = total + per_head(bias_ref)
        step = jnp.maximum(arg, 0.0) + jnp.log1p(jnp.exp(-jnp.abs(arg)))
        decay = -per_head(rate_ref) * step
        lower = causal.astype(F32)
        upper = (from_t <= from_s).astype(F32)
        pieces = []
        for i in range(2):
            part = decay[:, rows_of[i]]
            cum_row = jnp.dot(part, upper, preferred_element_type=F32, precision=lax.Precision.HIGHEST)
            cum_col = dot_t(lower, part, lax.Precision.HIGHEST)
            end = jnp.exp(jnp.broadcast_to(cum_row[:, STRETCH - 1 :], (8, HEAD_DIM)))
            pieces.append((cum_row, cum_col, step[:, rows_of[i]], end))
        return pieces

    def swap():
        return pltpu.make_async_remote_copy(
            src_ref=sx.at[c], dst_ref=sx.at[c], send_sem=xssem, recv_sem=xrsem,
            device_id=p["S"], device_id_type=MESH,
        )

    def swapped():
        return pltpu.make_async_remote_copy(
            src_ref=sx.at[1 - c], dst_ref=sx.at[1 - c], send_sem=xssem, recv_sem=xrsem,
            device_id=p["S"], device_id_type=MESH,
        )

    def split(value):
        high = value.astype(BF)
        return jnp.concatenate([high, (value - high.astype(F32)).astype(BF)], axis=0)

    def local_state(pieces):
        for i in range(2):
            cum_row, _, rate, _ = pieces[i]
            turned = brow[rows_of[i]].astype(F32).T
            weight = jnp.exp(cum_row[:, STRETCH - 1 :] - cum_row) * rate
            for h in range(LOCAL_HEADS):
                contrib[i, h] = dot((turned * weight[h : h + 1]).astype(BF), vrow[rows_of[i]])
        for h in range(LOCAL_HEADS):
            local = pieces[1][3][h : h + 1] * contrib[0, h] + contrib[1, h]
            sx[c, h * 128 : h * 128 + 128] = local.astype(BF)
        sx[c, 512:528] = split(pieces[0][3] * pieces[1][3])
        swap().start()

    def whole(ref, first):
        both = ref[first : first + 16].astype(F32)
        return both[:8] + both[8:]

    def chip_state():
        swapped().wait_recv()
        first, second = whole(sx.at[0], 512), whole(sx.at[1], 512)
        for k in range(2):
            at = pl.ds(pl.multiple_of(c * 256 + k * 128, 128), 128)
            decay = jnp.where(c == 0, second[k : k + 1], second[k + 2 : k + 3])
            both = decay * sx[0, at].astype(F32) + sx[1, at].astype(F32)
            stall[c, zy, k * 128 : k * 128 + 128] = both.astype(BF)
        stall[c, zy, 256:272] = split(first * second)

    def inside(pieces, h):
        for i in range(2):
            cum_row, cum_col, rate, _ = pieces[i]
            gram = dot_t(ct[h, rows_of[i]], brow[rows_of[i]])
            diff = cum_col[:, h : h + 1] - cum_row[h : h + 1]
            mix = jnp.exp(jnp.where(causal, diff, FAR_BELOW)) * (rate[h : h + 1] * SCALE) * gram
            value = vrow[rows_of[i]]
            inner[h, rows_of[i]] = dot(mix.astype(BF), value) + skip_ref[h] * value.astype(F32)

    def arriving():
        def advance(d, carried):
            blocks = [stall.at[k, d] for k in range(2)]
            total = whole(blocks[0], 256)
            return tuple(
                total[h : h + 1] * carried[h]
                + blocks[h // 2][h % 2 * 128 : h % 2 * 128 + 128].astype(F32)
                for h in range(LOCAL_HEADS)
            )

        zero = jnp.zeros((HEAD_DIM, HEAD_DIM), F32)
        carried = lax.fori_loop(0, zy, advance, (zero,) * LOCAL_HEADS)
        first = whole(sx.at[0], 512)
        return [
            jnp.where(
                c == 0, carried[h],
                first[h : h + 1] * carried[h] + sx[0, h * 128 : h * 128 + 128].astype(F32),
            )
            for h in range(LOCAL_HEADS)
        ]

    def student(pieces, incoming, h):
        for i in range(2):
            reach = jnp.exp(pieces[i][1]) * SCALE
            state = incoming[h] if i == 0 else pieces[0][3][h : h + 1] * incoming[h] + contrib[0, h]
            carried = dot(ct[h, rows_of[i]], state.astype(BF))
            out = inner[h, rows_of[i]] + reach[:, h : h + 1] * carried
            student_ref[rows_of[i], h * 128 : h * 128 + 128] = out.astype(BF)

    ones = jnp.ones((16, TOK), BF)

    def absorb(blocks, heads, diagonal=False):
        todo = [(b, h, i) for b in range(len(blocks)) for h in heads for i in range(TOK // HALF)]

        def scores(n):
            b, h, i = todo[n]
            keys = kall[(*blocks[b],)]
            keys = jnp.concatenate([keys[:, k * 128 : k * 128 + 128] for k in range(4)], axis=0)
            out = dot_t(keys, rq[h, i * HALF : i * HALF + HALF])
            if diagonal:
                at_u = lax.broadcasted_iota(jnp.int32, out.shape, 0)
                at_t = lax.broadcasted_iota(jnp.int32, out.shape, 1) + i * HALF
                out = jnp.where(at_u <= at_t, out, FAR_BELOW)
            return out

        found = {n: scores(n) for n in range(min(2, len(todo)))}
        ready = None
        for n in range(len(todo) + 1):
            now = None
            if n + 2 < len(todo):
                found[n + 2] = scores(n + 2)
            if n < len(todo):
                b, h, i = todo[n]
                cols = slice(i * HALF, i * HALF + HALF)
                score = found.pop(n)
                high = jnp.max(score, axis=0, keepdims=True)
                if diagonal:
                    peak, shrink = high, None
                else:
                    before = top[h, 0:1, cols]
                    peak = jnp.maximum(before, high)
                    shrink = jnp.exp2(before - peak)
                now = (b, h, cols, jnp.exp2(score - peak).astype(BF), shrink)
                top[h, 0:1, cols] = peak
            if ready is not None:
                b, h, cols, weights, shrink = ready
                mixed = dot(jnp.concatenate([vall[(*blocks[b],)], ones], axis=0), weights)
                acc[h, :, cols] = mixed if diagonal else mixed + acc[h, :, cols] * shrink
            ready = now

    def own_part(heads, part):
        if part == 0:
            absorb([(c, zy)], heads, True)
            pl.when(c == 1)(lambda: absorb([(0, zy)], heads))
            return

        def visit(j, carry):
            absorb([(0, j), (1, j)], heads)
            return carry

        lax.fori_loop(zh * 4, zy, visit, 0)

    def low_part(heads, part):
        first = part * 2

        def both():
            if len(heads) > 1:
                absorb([(0, first), (1, first)], heads)
                absorb([(0, first + 1), (1, first + 1)], heads)
            else:
                absorb([(k % 2, first + k // 2) for k in range(4)], heads)

        pl.when(zh == 1)(both)

    def teacher(h):
        done = acc[h]
        out = (done[:128] / done[128:129]).T
        teacher_ref[:, h * 128 : h * 128 + 128] = out.astype(BF)

    place("k")
    enter(["R", "L", "Z", "S", "G"], p)
    w["k"].ay()
    place("v")
    w["v"].az()
    w["v"].ay()
    place("q3")
    send_raw()
    place("q0")
    w["q0"].ay()
    w["k"].az()
    place("q1")
    place("q2")
    w["q1"].az()
    w["q1"].ay()
    w["q0"].az()
    w["q3"].az()
    w["v"].zs()
    pieces = decays()
    w["k"].zs()
    w["v"].f()
    w["v"].zf()
    w["k"].f()
    w["k"].zf()
    w["q1"].f()
    w["q2"].az()
    w["v"].s1()
    w["v"].s2()
    w["q0"].f()
    w["q1"].zs()
    w["k"].s1()
    arrange()
    w["k"].s2()
    w["q3"].ay()
    multiply("v")
    w["q1"].s1()
    multiply("k")
    w["q0"].s1()
    w["q1"].zf()
    w["q0"].zs()
    w["q1"].s2()
    settle("v")
    kept["v"].a()
    w["q0"].zf()
    multiply("q1")
    w["q3"].zs()
    settle("k")
    kept["v"].b()
    w["q0"].s2()
    local_state(pieces)
    kept["k"].a()
    multiply("q0")
    w["q3"].f()
    kept["v"].c()
    w["q3"].zf()
    kept["k"].b()
    kept["v"].near()
    w["q3"].s1()
    w["q2"].ay()
    w["q2"].zs()
    w["q3"].s2()
    settle("q1")
    inside(pieces, 1)
    kept["k"].c()
    chip_state()
    kept["s"].a()
    settle("q0")
    inside(pieces, 0)
    multiply("q3")
    kept["k"].near()
    own_part([0, 1], 0)
    kept["v"].d()
    w["q2"].f()
    w["q2"].zf()
    own_part([0, 1], 1)
    w["q2"].s2()
    w["q2"].s1()
    kept["s"].b()
    kept["v"].e()
    settle("q3")
    own_part([3], 0)
    inside(pieces, 3)
    kept["k"].d()
    own_part([3], 1)
    kept["s"].c()
    multiply("q2")
    kept["k"].e()
    low_part([0, 1], 0)
    kept["s"].d()
    low_part([0, 1], 1)
    teacher(1)
    low_part([3], 0)
    low_part([3], 1)
    settle("q2")
    inside(pieces, 2)
    kept["s"].e()
    own_part([2], 0)
    low_part([2], 1)
    kept["s"].near()
    own_part([2], 1)
    incoming = arriving()
    student(pieces, incoming, 1)
    student(pieces, incoming, 0)
    teacher(0)
    student(pieces, incoming, 3)
    low_part([2], 0)
    teacher(2)
    teacher(3)
    student(pieces, incoming, 2)
    for name in KINDS:
        w[name].sent()
        for cp in tiles(name):
            cp.wait_send()
    for d in range(3):
        raw_tile(d).wait_send()
    for name in kept:
        kept[name].sent()
    swap().wait_send()


def tables():
    half = HEAD_DIM // 2
    freq = ROPE_BASE ** (-2.0 * np.arange(half) / HEAD_DIM)
    freq = np.concatenate([freq, freq])
    near = np.arange(TOK)[:, None] * freq[None]
    base = (np.arange(16) * TOK)[:, None] * freq[None]
    return (
        np.stack([np.cos(near), np.sin(near)]).astype(np.float32),
        np.stack([np.cos(base), np.sin(base)]).astype(np.float32),
    )


def body(layer_input, attn_weight, rate_weight, rate_bias, decay_rate, skip_gain):
    vmem = pl.BlockSpec(memory_space=pltpu.VMEM)
    smem = pl.BlockSpec(memory_space=pltpu.SMEM)
    dma = pltpu.SemaphoreType.DMA
    near, base = tables()
    heads = (LOCAL_HEADS, TOK, HEAD_DIM)
    return pl.pallas_call(
        window_kernel,
        name="window",
        out_shape=(
            jax.ShapeDtypeStruct((TOK, 512), BF),
            jax.ShapeDtypeStruct((TOK, 512), BF),
        ),
        in_specs=[vmem] * 5 + [smem] * 3,
        out_specs=(vmem, vmem),
        scratch_shapes=[
            pltpu.VMEM((2, 2, 8, 128, 256), BF),
            pltpu.VMEM((4, 2, 8, 128, 512), BF),
            pltpu.VMEM((2, TOK, 1024), BF),
            pltpu.VMEM((2, 2, TOK, 128), F32),
            pltpu.VMEM((2, 4, TOK, 128), F32),
            pltpu.VMEM((4, 4, TOK, 128), BF),
            pltpu.VMEM((4, 3, TOK, 128), BF),
            pltpu.VMEM((2, 2, TOK, 128), BF),
            pltpu.VMEM((2, 3, TOK, 128), BF),
            pltpu.VMEM((4, 8, TOK), F32),
            pltpu.VMEM((3, 8, TOK), F32),
            pltpu.VMEM((2, 8, 128, TOK), BF),
            pltpu.VMEM((2, 8, 128, TOK), BF),
            pltpu.VMEM((2, 8, 272, 128), BF),
            pltpu.VMEM((2, 528, 128), BF),
            pltpu.VMEM(heads, BF),
            pltpu.VMEM(heads, BF),
            pltpu.VMEM((TOK, HEAD_DIM), BF),
            pltpu.VMEM((TOK, HEAD_DIM), BF),
            pltpu.VMEM((2, LOCAL_HEADS, HEAD_DIM, HEAD_DIM), F32),
            pltpu.VMEM(heads, F32),
            pltpu.VMEM((LOCAL_HEADS, 144, TOK), F32),
            pltpu.VMEM((LOCAL_HEADS, 8, TOK), F32),
            dma((len(KINDS), COPIES)),
            dma((len(KINDS), COPIES)),
            dma((len(KINDS) + 1, 3)),
            dma((len(KINDS) + 1, 3)),
            dma((3, COPIES)),
            dma((3, COPIES)),
            dma,
            dma,
        ],
        compiler_params=pltpu.CompilerParams(
            collective_id=0, has_side_effects=True, vmem_limit_bytes=58 * 2**20
        ),
    )(
        layer_input, attn_weight.reshape(128, 2560), rate_weight.T, jnp.asarray(near),
        jnp.asarray(base), rate_bias, decay_rate, skip_gain,
    )


def solution(mesh):
    placed = (
        P("seq", "grp"),
        P(("grp", "seq"), "mdl", None),
        P("grp", "mdl"),
        P(("mdl", "grp")),
        P(("mdl", "grp")),
        P(("mdl", "grp")),
    )
    return jax.shard_map(
        body,
        mesh=mesh,
        in_specs=placed,
        out_specs=(P("seq", ("mdl", "grp")), P("seq", ("mdl", "grp"))),
        check_vma=False,
    )
```

```python
import functools
import math

import jax
import jax.numpy as jnp
import numpy as np
from jax import lax
from jax.experimental import pallas as pl
from jax.experimental.pallas import tpu as pltpu
from jax.sharding import PartitionSpec as P

HEAD_DIM = 128
STRETCH = 256
ROPE_BASE = 500000.0
FAR_BELOW = -1e30
TOK = 512
LOCAL_HEADS = 4
KINDS = ("k", "v", "q0", "q1", "q2", "q3")
COPIES = 11
HALF = 256
SCALE = HEAD_DIM**-0.5
LOG2E = math.log2(math.e)
MESH = pl.DeviceIdType.MESH
BF = jnp.bfloat16
F32 = jnp.float32


def places():
    g, s, m = lax.axis_index("grp"), lax.axis_index("seq"), lax.axis_index("mdl")
    zh, y, c = s // 8, (s // 2) % 4, s % 2

    def seq(zh, y, c):
        return zh * 8 + y * 2 + c

    up, down, far = lax.rem(y + 1, 4), lax.rem(y + 3, 4), lax.rem(y + 2, 4)
    return {
        "g": g, "s": s, "zh": zh, "y": y, "c": c,
        "zy": zh * 4 + y,
        "up": up, "down": down, "far": far,
        "R": (g, seq(zh, up, c), m),
        "L": (g, seq(zh, down, c), m),
        "Z": (g, seq(1 - zh, y, c), m),
        "S": (g, seq(zh, y, 1 - c), m),
        "G": [(lax.rem(g + d, 4), s, m) for d in (1, 2, 3)],
    }


def enter(names, p):
    bar = pltpu.get_barrier_semaphore()
    targets = []
    for name in names:
        targets += p[name] if name == "G" else [p[name]]
    for dev in targets:
        pl.semaphore_signal(bar, inc=1, device_id=dev, device_id_type=MESH)
    pl.semaphore_wait(bar, len(targets))


class Gather:
    def __init__(self, buf, ssem, rsem, p, half):
        self.buf, self.ssem, self.rsem, self.p = buf, ssem, rsem, p
        self.rows, self.half = buf.shape[-2], half

    def remote(self, k, ref, dev):
        return pltpu.make_async_remote_copy(
            src_ref=ref, dst_ref=ref, send_sem=self.ssem.at[k], recv_sem=self.rsem.at[k],
            device_id=dev, device_id_type=MESH,
        )

    def copy(self, k, dev, zy, first=None, count=None):
        c = self.p["c"]
        ref = self.buf.at[c, zy] if first is None else self.buf.at[c, zy, pl.ds(first, count)]
        return self.remote(k, ref, dev)

    def four(self, k, own, core):
        return self.remote(k, self.buf.at[core, pl.ds(self.base(own), 4)], self.p["S"])

    def base(self, own):
        return (self.p["zh"] if own else 1 - self.p["zh"]) * 4

    def spread(self, own):
        p, k = self.p, 0 if own else 5
        at = self.base(own) + p["y"]
        return self.copy(k, p["R"], at), self.copy(k + 1, p["L"], at)

    def arrive(self, own):
        p, k = self.p, 0 if own else 5
        return (
            self.copy(k, p["R"], self.base(own) + p["down"]),
            self.copy(k + 1, p["L"], self.base(own) + p["up"]),
        )

    def pair(self, own, left, right):
        p, k = self.p, 2 if own else 7
        return (
            self.copy(k, p["R"], self.base(own) + left, 0, self.half),
            self.copy(k + 1, p["L"], self.base(own) + right, self.half, self.rows - self.half),
        )

    def forward(self, own):
        return self.pair(own, self.p["down"], self.p["up"])

    def halves(self, own):
        return self.pair(own, self.p["far"], self.p["far"])

    def across(self, own):
        return self.copy(4, self.p["Z"], self.base(own) + self.p["y"])

    def ay(self):
        for cp in self.spread(True):
            cp.start()

    def az(self):
        self.across(True).start()

    def pass_on(self, own):
        for got, on in zip(self.arrive(own), self.forward(own)):
            got.wait_recv()
            on.start()

    def f(self):
        self.pass_on(True)

    def zs(self):
        self.across(False).wait_recv()
        for cp in self.spread(False):
            cp.start()

    def finish(self, own):
        for cp in self.halves(own):
            cp.wait_recv()
        self.four(9 if own else 10, own, self.p["c"]).start()

    def s1(self):
        self.finish(True)

    def zf(self):
        self.pass_on(False)

    def s2(self):
        self.finish(False)

    def e(self):
        for own in (True, False):
            self.four(9 if own else 10, own, 1 - self.p["c"]).wait_recv()

    def sent(self):
        for own in (True, False):
            for cp in (*self.spread(own), *self.forward(own)):
                cp.wait_send()
            self.four(9 if own else 10, own, self.p["c"]).wait_send()
        self.across(True).wait_send()


class Earlier(Gather):
    def low(self, f):
        pl.when(self.p["zh"] == 0)(f)

    def high(self, f):
        pl.when(self.p["zh"] == 1)(f)

    def a(self):
        self.low(self.az)
        self.ay()

    def b(self):
        self.f()

    def c(self):
        self.s1()

    def near(self):
        self.four(9, True, 1 - self.p["c"]).wait_recv()

    def zs(self):
        self.high(super().zs)

    def zf(self):
        self.high(super().zf)

    def d(self):
        self.high(self.s2)

    def e(self):
        self.high(lambda: self.four(10, False, 1 - self.p["c"]).wait_recv())

    def sent(self):
        for cp in (*self.spread(True), *self.forward(True)):
            cp.wait_send()
        self.four(9, True, self.p["c"]).wait_send()
        self.low(lambda: self.across(True).wait_send())

        def other():
            for cp in (*self.spread(False), *self.forward(False)):
                cp.wait_send()
            self.four(10, False, self.p["c"]).wait_send()

        self.high(other)


def dot(a, b):
    return jnp.dot(a, b, preferred_element_type=F32)


def dot_t(a, b, precision=None):
    return lax.dot_general(
        a, b, (((1,), (1,)), ((), ())), preferred_element_type=F32, precision=precision
    )


def window_kernel(
    x_ref, w_ref, rate_w_ref, near_ref, base_ref, bias_ref, rate_ref, skip_ref,
    teacher_ref, student_ref,
    wkv, wq, xp, own_kv, own_q, qsend, qrecv, kvsend, kvrecv, rawsend, rawrecv,
    kall, vall, stall, sx, rq, ct, vrow, brow, contrib, inner, acc, top,
    wssem, wrsem, gssem, grsem, kssem, krsem, xssem, xrsem,
):
    p = places()
    g, s, zh, c, zy = p["g"], p["s"], p["zh"], p["c"], p["zy"]
    w = {}
    for n, name in enumerate(KINDS):
        buf = wkv.at[n] if n < 2 else wq.at[n - 2]
        w[name] = Gather(buf, wssem.at[n], wrsem.at[n], p, 64)
    kept = {
        name: Earlier(buf, kssem.at[n], krsem.at[n], p, half)
        for n, (name, buf, half) in enumerate((("k", kall, 64), ("v", vall, 64), ("s", stall, 128)))
    }

    def place(name):
        if name in "kv":
            n = "kv".index(name)
            for k in range(2):
                first = k * 1280 + 1024 + n * 128
                wkv[n, c, zy, :, k * 128 : k * 128 + 128] = w_ref[:, first : first + 128]
            return
        n = int(name[1])
        for d in range(4):
            first = d // 2 * 1280 + d % 2 * 512 + n * 128
            wq[n, c, zy, :, d * 128 : d * 128 + 128] = w_ref[:, first : first + 128]

    def tile(source, target, k, d):
        return pltpu.make_async_remote_copy(
            src_ref=source, dst_ref=target, send_sem=gssem.at[k, d], recv_sem=grsem.at[k, d],
            device_id=p["G"][d], device_id_type=MESH,
        )

    def raw_tile(d):
        return tile(rawsend.at[lax.rem(g + d + 1, 4)], rawrecv.at[d], len(KINDS), d)

    def tiles(name):
        k = KINDS.index(name)
        if k < 2:
            return [
                tile(kvsend.at[k, lax.rem(g + d + 1, 4) // 2], kvrecv.at[k, d], k, d) for d in range(3)
            ]
        return [
            tile(qsend.at[k - 2, lax.rem(g + d + 1, 4)], qrecv.at[k - 2, d], k, d) for d in range(3)
        ]

    def send_raw():
        raw = dot_t(rate_w_ref[...], x_ref[...])
        for d in range(4):
            rawsend[d] = jnp.concatenate([raw[4 * d : 4 * d + 4], raw[4 * d : 4 * d + 4]], axis=0)
        for d in range(3):
            raw_tile(d).start()

    def arrange():
        for core in range(2):
            for at in range(8):
                src = (at * 2 + core) * 128
                xp[core, :, at * 128 : at * 128 + 128] = x_ref[:, src : src + 128]

    def rotate(u):
        near_c, near_s = near_ref[0], near_ref[1]
        far_c, far_s = base_ref[0, pl.ds(s, 1), :], base_ref[1, pl.ds(s, 1), :]
        lane = lax.broadcasted_iota(jnp.int32, (1, HEAD_DIM), 1)
        sign = jnp.where(lane < HEAD_DIM // 2, -1.0, 1.0)
        cosine = near_c * far_c - near_s * far_s
        sine = (near_s * far_c + near_c * far_s) * sign
        return u * cosine + pltpu.roll(u, HEAD_DIM // 2, 1) * sine

    def multiply(name):
        w[name].e()
        k = KINDS.index(name)
        buf = wkv.at[k] if k < 2 else wq.at[k - 2]
        out = sum(dot(xp[core], buf[core].reshape(1024, buf.shape[-1])) for core in range(2))
        for d in range(buf.shape[-1] // 128):
            part = out[:, d * 128 : d * 128 + 128]
            if k < 2:
                own_kv[k, d] = part
                kvsend[k, d] = part.astype(BF)
            else:
                own_q[k % 2, d] = part
                qsend[k - 2, d] = part.astype(BF)
        for cp in tiles(name):
            cp.start()

    def settle(name):
        k = KINDS.index(name)
        for cp in tiles(name):
            cp.wait_recv()
        got = own_kv[k, g // 2] if k < 2 else own_q[k % 2, g]
        for d in range(3):
            got = got + (kvrecv[k, d] if k < 2 else qrecv[k - 2, d]).astype(F32)
        if name == "k":
            turned = rotate(got).astype(BF)
            for i in range(4):
                kall[c, zy, :, i * 128 : i * 128 + 128] = turned[i * 128 : i * 128 + 128]
            brow[...] = got.astype(BF)
        elif name == "v":
            vall[c, zy] = got.T.astype(BF)
            vrow[...] = got.astype(BF)
        else:
            ct[k - 2] = got.astype(BF)
            rq[k - 2] = (rotate(got) * (SCALE * LOG2E)).astype(BF)

    row = lax.broadcasted_iota(jnp.int32, (8, TOK), 0)

    def per_head(ref):
        out = jnp.full((8, TOK), ref[0], F32)
        for h in range(1, LOCAL_HEADS):
            out = jnp.where(row % LOCAL_HEADS == h, ref[h], out)
        return out

    from_t = lax.broadcasted_iota(jnp.int32, (STRETCH, STRETCH), 0)
    from_s = lax.broadcasted_iota(jnp.int32, (STRETCH, STRETCH), 1)
    causal = from_s <= from_t
    rows_of = [slice(i * STRETCH, (i + 1) * STRETCH) for i in range(2)]

    def decays():
        total = rawsend[g]
        for d in range(3):
            raw_tile(d).wait_recv()
            total = total + rawrecv[d]
        arg = total + per_head(bias_ref)
        step = jnp.maximum(arg, 0.0) + jnp.log1p(jnp.exp(-jnp.abs(arg)))
        decay = -per_head(rate_ref) * step
        lower = causal.astype(F32)
        upper = (from_t <= from_s).astype(F32)
        pieces = []
        for i in range(2):
            part = decay[:, rows_of[i]]
            cum_row = jnp.dot(part, upper, preferred_element_type=F32, precision=lax.Precision.HIGHEST)
            cum_col = dot_t(lower, part, lax.Precision.HIGHEST)
            end = jnp.exp(jnp.broadcast_to(cum_row[:, STRETCH - 1 :], (8, HEAD_DIM)))
            pieces.append((cum_row, cum_col, step[:, rows_of[i]], end))
        return pieces

    def swap():
        return pltpu.make_async_remote_copy(
            src_ref=sx.at[c], dst_ref=sx.at[c], send_sem=xssem, recv_sem=xrsem,
            device_id=p["S"], device_id_type=MESH,
        )

    def swapped():
        return pltpu.make_async_remote_copy(
            src_ref=sx.at[1 - c], dst_ref=sx.at[1 - c], send_sem=xssem, recv_sem=xrsem,
            device_id=p["S"], device_id_type=MESH,
        )

    def split(value):
        high = value.astype(BF)
        return jnp.concatenate([high, (value - high.astype(F32)).astype(BF)], axis=0)

    def local_state(pieces):
        for i in range(2):
            cum_row, _, rate, _ = pieces[i]
            turned = brow[rows_of[i]].astype(F32).T
            weight = jnp.exp(cum_row[:, STRETCH - 1 :] - cum_row) * rate
            for h in range(LOCAL_HEADS):
                contrib[i, h] = dot((turned * weight[h : h + 1]).astype(BF), vrow[rows_of[i]])
        for h in range(LOCAL_HEADS):
            local = pieces[1][3][h : h + 1] * contrib[0, h] + contrib[1, h]
            sx[c, h * 128 : h * 128 + 128] = local.astype(BF)
        sx[c, 512:528] = split(pieces[0][3] * pieces[1][3])
        swap().start()

    def whole(ref, first):
        both = ref[first : first + 16].astype(F32)
        return both[:8] + both[8:]

    def chip_state():
        swapped().wait_recv()
        first, second = whole(sx.at[0], 512), whole(sx.at[1], 512)
        for k in range(2):
            at = pl.ds(pl.multiple_of(c * 256 + k * 128, 128), 128)
            decay = jnp.where(c == 0, second[k : k + 1], second[k + 2 : k + 3])
            both = decay * sx[0, at].astype(F32) + sx[1, at].astype(F32)
            stall[c, zy, k * 128 : k * 128 + 128] = both.astype(BF)
        stall[c, zy, 256:272] = split(first * second)

    def inside(pieces, h):
        for i in range(2):
            cum_row, cum_col, rate, _ = pieces[i]
            gram = dot_t(ct[h, rows_of[i]], brow[rows_of[i]])
            diff = cum_col[:, h : h + 1] - cum_row[h : h + 1]
            mix = jnp.exp(jnp.where(causal, diff, FAR_BELOW)) * (rate[h : h + 1] * SCALE) * gram
            value = vrow[rows_of[i]]
            inner[h, rows_of[i]] = dot(mix.astype(BF), value) + skip_ref[h] * value.astype(F32)

    def arriving():
        def advance(d, carried):
            blocks = [stall.at[k, d] for k in range(2)]
            total = whole(blocks[0], 256)
            return tuple(
                total[h : h + 1] * carried[h]
                + blocks[h // 2][h % 2 * 128 : h % 2 * 128 + 128].astype(F32)
                for h in range(LOCAL_HEADS)
            )

        zero = jnp.zeros((HEAD_DIM, HEAD_DIM), F32)
        carried = lax.fori_loop(0, zy, advance, (zero,) * LOCAL_HEADS)
        first = whole(sx.at[0], 512)
        return [
            jnp.where(
                c == 0, carried[h],
                first[h : h + 1] * carried[h] + sx[0, h * 128 : h * 128 + 128].astype(F32),
            )
            for h in range(LOCAL_HEADS)
        ]

    def student(pieces, incoming, h):
        for i in range(2):
            reach = jnp.exp(pieces[i][1]) * SCALE
            state = incoming[h] if i == 0 else pieces[0][3][h : h + 1] * incoming[h] + contrib[0, h]
            carried = dot(ct[h, rows_of[i]], state.astype(BF))
            out = inner[h, rows_of[i]] + reach[:, h : h + 1] * carried
            student_ref[rows_of[i], h * 128 : h * 128 + 128] = out.astype(BF)

    ones = jnp.ones((16, TOK), BF)

    def absorb(blocks, heads, diagonal=False):
        todo = [(b, h, i) for b in range(len(blocks)) for h in heads for i in range(TOK // HALF)]

        def scores(n):
            b, h, i = todo[n]
            keys = kall[(*blocks[b],)]
            keys = jnp.concatenate([keys[:, k * 128 : k * 128 + 128] for k in range(4)], axis=0)
            out = dot_t(keys, rq[h, i * HALF : i * HALF + HALF])
            if diagonal:
                at_u = lax.broadcasted_iota(jnp.int32, out.shape, 0)
                at_t = lax.broadcasted_iota(jnp.int32, out.shape, 1) + i * HALF
                out = jnp.where(at_u <= at_t, out, FAR_BELOW)
            return out

        found = {n: scores(n) for n in range(min(2, len(todo)))}
        ready = None
        for n in range(len(todo) + 1):
            now = None
            if n + 2 < len(todo):
                found[n + 2] = scores(n + 2)
            if n < len(todo):
                b, h, i = todo[n]
                cols = slice(i * HALF, i * HALF + HALF)
                score = found.pop(n)
                high = jnp.max(score, axis=0, keepdims=True)
                if diagonal:
                    peak, shrink = high, None
                else:
                    before = top[h, 0:1, cols]
                    peak = jnp.maximum(before, high)
                    shrink = jnp.exp2(before - peak)
                now = (b, h, cols, jnp.exp2(score - peak).astype(BF), shrink)
                top[h, 0:1, cols] = peak
            if ready is not None:
                b, h, cols, weights, shrink = ready
                mixed = dot(jnp.concatenate([vall[(*blocks[b],)], ones], axis=0), weights)
                acc[h, :, cols] = mixed if diagonal else mixed + acc[h, :, cols] * shrink
            ready = now

    def own_part(heads, part):
        if part == 0:
            absorb([(c, zy)], heads, True)
            pl.when(c == 1)(lambda: absorb([(0, zy)], heads))
            return

        def visit(j, carry):
            absorb([(0, j), (1, j)], heads)
            return carry

        lax.fori_loop(zh * 4, zy, visit, 0)

    def low_part(heads, part):
        first = part * 2

        def both():
            if len(heads) > 1:
                absorb([(0, first), (1, first)], heads)
                absorb([(0, first + 1), (1, first + 1)], heads)
            else:
                absorb([(k % 2, first + k // 2) for k in range(4)], heads)

        pl.when(zh == 1)(both)

    def teacher(h):
        done = acc[h]
        out = (done[:128] / done[128:129]).T
        teacher_ref[:, h * 128 : h * 128 + 128] = out.astype(BF)

    place("k")
    enter(["R", "L", "Z", "S", "G"], p)
    w["k"].ay()
    w["k"].az()
    place("v")
    w["v"].ay()
    place("q0")
    w["q0"].ay()
    send_raw()
    place("q1")
    w["v"].az()
    w["k"].f()
    w["v"].f()
    pieces = decays()
    w["k"].zs()
    w["q0"].az()
    w["q1"].ay()
    place("q2")
    w["v"].zs()
    w["q1"].az()
    w["k"].s1()
    w["q0"].f()
    w["v"].s1()
    w["k"].zf()
    w["v"].zf()
    w["q1"].f()
    w["q2"].ay()
    w["q0"].zs()
    place("q3")
    w["q2"].az()
    w["k"].s2()
    w["v"].s2()
    w["q1"].s1()
    arrange()
    multiply("v")
    w["q2"].f()
    w["q1"].zs()
    w["q3"].az()
    w["q0"].zf()
    w["q0"].s1()
    multiply("k")
    w["q2"].s1()
    w["q2"].zs()
    w["q1"].zf()
    settle("v")
    kept["v"].a()
    w["q0"].s2()
    multiply("q0")
    w["q2"].zf()
    w["q1"].s2()
    settle("k")
    kept["k"].a()
    local_state(pieces)
    chip_state()
    w["q2"].s2()
    kept["v"].b()
    w["q3"].ay()
    multiply("q1")
    kept["k"].b()
    settle("q0")
    multiply("q2")
    w["q3"].zs()
    kept["v"].c()
    kept["v"].zs()
    inside(pieces, 0)
    w["q3"].f()
    kept["k"].c()
    kept["k"].zs()
    settle("q1")
    inside(pieces, 1)
    kept["k"].near()
    kept["v"].near()
    w["q3"].zf()
    own_part([0, 1], 0)
    kept["v"].zf()
    own_part([0, 1], 1)
    kept["k"].zf()
    kept["s"].a()
    settle("q2")
    w["q3"].s1()
    own_part([2], 0)
    w["q3"].s2()
    kept["v"].d()
    own_part([2], 1)
    kept["k"].d()
    kept["s"].b()
    inside(pieces, 2)
    kept["v"].e()
    kept["s"].zs()
    multiply("q3")
    kept["k"].e()
    low_part([2], 0)
    kept["s"].zf()
    kept["s"].c()
    low_part([0, 1], 1)
    kept["s"].d()
    low_part([0, 1], 0)
    settle("q3")
    own_part([3], 0)
    low_part([3], 1)
    low_part([3], 0)
    own_part([3], 1)
    kept["s"].e()
    low_part([2], 1)
    teacher(2)
    kept["s"].near()
    incoming = arriving()
    student(pieces, incoming, 1)
    teacher(1)
    inside(pieces, 3)
    student(pieces, incoming, 3)
    teacher(3)
    student(pieces, incoming, 0)
    teacher(0)
    student(pieces, incoming, 2)
    for name in KINDS:
        w[name].sent()
        for cp in tiles(name):
            cp.wait_send()
    for d in range(3):
        raw_tile(d).wait_send()
    for name in kept:
        kept[name].sent()
    swap().wait_send()


def tables():
    half = HEAD_DIM // 2
    freq = ROPE_BASE ** (-2.0 * np.arange(half) / HEAD_DIM)
    freq = np.concatenate([freq, freq])
    near = np.arange(TOK)[:, None] * freq[None]
    base = (np.arange(16) * TOK)[:, None] * freq[None]
    return (
        np.stack([np.cos(near), np.sin(near)]).astype(np.float32),
        np.stack([np.cos(base), np.sin(base)]).astype(np.float32),
    )


def body(layer_input, attn_weight, rate_weight, rate_bias, decay_rate, skip_gain):
    vmem = pl.BlockSpec(memory_space=pltpu.VMEM)
    smem = pl.BlockSpec(memory_space=pltpu.SMEM)
    dma = pltpu.SemaphoreType.DMA
    near, base = tables()
    heads = (LOCAL_HEADS, TOK, HEAD_DIM)
    return pl.pallas_call(
        window_kernel,
        name="window",
        out_shape=(
            jax.ShapeDtypeStruct((TOK, 512), BF),
            jax.ShapeDtypeStruct((TOK, 512), BF),
        ),
        in_specs=[vmem] * 5 + [smem] * 3,
        out_specs=(vmem, vmem),
        scratch_shapes=[
            pltpu.VMEM((2, 2, 8, 128, 256), BF),
            pltpu.VMEM((4, 2, 8, 128, 512), BF),
            pltpu.VMEM((2, TOK, 1024), BF),
            pltpu.VMEM((2, 2, TOK, 128), F32),
            pltpu.VMEM((2, 4, TOK, 128), F32),
            pltpu.VMEM((4, 4, TOK, 128), BF),
            pltpu.VMEM((4, 3, TOK, 128), BF),
            pltpu.VMEM((2, 2, TOK, 128), BF),
            pltpu.VMEM((2, 3, TOK, 128), BF),
            pltpu.VMEM((4, 8, TOK), F32),
            pltpu.VMEM((3, 8, TOK), F32),
            pltpu.VMEM((2, 8, 128, TOK), BF),
            pltpu.VMEM((2, 8, 128, TOK), BF),
            pltpu.VMEM((2, 8, 272, 128), BF),
            pltpu.VMEM((2, 528, 128), BF),
            pltpu.VMEM(heads, BF),
            pltpu.VMEM(heads, BF),
            pltpu.VMEM((TOK, HEAD_DIM), BF),
            pltpu.VMEM((TOK, HEAD_DIM), BF),
            pltpu.VMEM((2, LOCAL_HEADS, HEAD_DIM, HEAD_DIM), F32),
            pltpu.VMEM(heads, F32),
            pltpu.VMEM((LOCAL_HEADS, 144, TOK), F32),
            pltpu.VMEM((LOCAL_HEADS, 8, TOK), F32),
            dma((len(KINDS), COPIES)),
            dma((len(KINDS), COPIES)),
            dma((len(KINDS) + 1, 3)),
            dma((len(KINDS) + 1, 3)),
            dma((3, COPIES)),
            dma((3, COPIES)),
            dma,
            dma,
        ],
        compiler_params=pltpu.CompilerParams(
            collective_id=0, has_side_effects=True, vmem_limit_bytes=58 * 2**20
        ),
    )(
        layer_input, attn_weight.reshape(128, 2560), rate_weight.T, jnp.asarray(near),
        jnp.asarray(base), rate_bias, decay_rate, skip_gain,
    )


def solution(mesh):
    placed = (
        P("seq", "grp"),
        P(("grp", "seq"), "mdl", None),
        P("grp", "mdl"),
        P(("mdl", "grp")),
        P(("mdl", "grp")),
        P(("mdl", "grp")),
    )
    return jax.shard_map(
        body,
        mesh=mesh,
        in_specs=placed,
        out_specs=(P("seq", ("mdl", "grp")), P("seq", ("mdl", "grp"))),
        check_vma=False,
    )
```

```python
import functools
import math

import jax
import jax.numpy as jnp
import numpy as np
from jax import lax
from jax.experimental import pallas as pl
from jax.experimental.pallas import tpu as pltpu
from jax.sharding import PartitionSpec as P

HEAD_DIM = 128
STRETCH = 256
ROPE_BASE = 500000.0
FAR_BELOW = -1e30
TOK = 512
LOCAL_HEADS = 4
KINDS = ("k", "v", "q0", "q1", "q2", "q3")
COPIES = 11
HALF = 256
SCALE = HEAD_DIM**-0.5
LOG2E = math.log2(math.e)
MESH = pl.DeviceIdType.MESH
BF = jnp.bfloat16
F32 = jnp.float32


def places():
    g, s, m = lax.axis_index("grp"), lax.axis_index("seq"), lax.axis_index("mdl")
    zh, y, c = s // 8, (s // 2) % 4, s % 2

    def seq(zh, y, c):
        return zh * 8 + y * 2 + c

    up, down, far = lax.rem(y + 1, 4), lax.rem(y + 3, 4), lax.rem(y + 2, 4)
    return {
        "g": g, "s": s, "zh": zh, "y": y, "c": c,
        "zy": zh * 4 + y,
        "up": up, "down": down, "far": far,
        "R": (g, seq(zh, up, c), m),
        "L": (g, seq(zh, down, c), m),
        "Z": (g, seq(1 - zh, y, c), m),
        "S": (g, seq(zh, y, 1 - c), m),
        "G": [(lax.rem(g + d, 4), s, m) for d in (1, 2, 3)],
    }


def enter(names, p):
    bar = pltpu.get_barrier_semaphore()
    targets = []
    for name in names:
        targets += p[name] if name == "G" else [p[name]]
    for dev in targets:
        pl.semaphore_signal(bar, inc=1, device_id=dev, device_id_type=MESH)
    pl.semaphore_wait(bar, len(targets))


class Gather:
    def __init__(self, buf, ssem, rsem, p, half):
        self.buf, self.ssem, self.rsem, self.p = buf, ssem, rsem, p
        self.rows, self.half = buf.shape[-2], half

    def remote(self, k, ref, dev):
        return pltpu.make_async_remote_copy(
            src_ref=ref, dst_ref=ref, send_sem=self.ssem.at[k], recv_sem=self.rsem.at[k],
            device_id=dev, device_id_type=MESH,
        )

    def copy(self, k, dev, zy, first=None, count=None):
        c = self.p["c"]
        ref = self.buf.at[c, zy] if first is None else self.buf.at[c, zy, pl.ds(first, count)]
        return self.remote(k, ref, dev)

    def four(self, k, own, core):
        return self.remote(k, self.buf.at[core, pl.ds(self.base(own), 4)], self.p["S"])

    def base(self, own):
        return (self.p["zh"] if own else 1 - self.p["zh"]) * 4

    def spread(self, own):
        p, k = self.p, 0 if own else 5
        at = self.base(own) + p["y"]
        return self.copy(k, p["R"], at), self.copy(k + 1, p["L"], at)

    def arrive(self, own):
        p, k = self.p, 0 if own else 5
        return (
            self.copy(k, p["R"], self.base(own) + p["down"]),
            self.copy(k + 1, p["L"], self.base(own) + p["up"]),
        )

    def pair(self, own, left, right):
        p, k = self.p, 2 if own else 7
        return (
            self.copy(k, p["R"], self.base(own) + left, 0, self.half),
            self.copy(k + 1, p["L"], self.base(own) + right, self.half, self.rows - self.half),
        )

    def forward(self, own):
        return self.pair(own, self.p["down"], self.p["up"])

    def halves(self, own):
        return self.pair(own, self.p["far"], self.p["far"])

    def across(self, own):
        return self.copy(4, self.p["Z"], self.base(own) + self.p["y"])

    def ay(self):
        for cp in self.spread(True):
            cp.start()

    def az(self):
        self.across(True).start()

    def pass_on(self, own):
        for got, on in zip(self.arrive(own), self.forward(own)):
            got.wait_recv()
            on.start()

    def f(self):
        self.pass_on(True)

    def zs(self):
        self.across(False).wait_recv()
        for cp in self.spread(False):
            cp.start()

    def finish(self, own):
        for cp in self.halves(own):
            cp.wait_recv()
        self.four(9 if own else 10, own, self.p["c"]).start()

    def s1(self):
        self.finish(True)

    def zf(self):
        self.pass_on(False)

    def s2(self):
        self.finish(False)

    def e(self):
        for own in (True, False):
            self.four(9 if own else 10, own, 1 - self.p["c"]).wait_recv()

    def sent(self):
        for own in (True, False):
            for cp in (*self.spread(own), *self.forward(own)):
                cp.wait_send()
            self.four(9 if own else 10, own, self.p["c"]).wait_send()
        self.across(True).wait_send()


class Earlier(Gather):
    def low(self, f):
        pl.when(self.p["zh"] == 0)(f)

    def high(self, f):
        pl.when(self.p["zh"] == 1)(f)

    def a(self):
        self.low(self.az)
        self.ay()

    def b(self):
        self.f()

    def c(self):
        self.s1()

    def near(self):
        self.four(9, True, 1 - self.p["c"]).wait_recv()

    def zs(self):
        self.high(super().zs)

    def zf(self):
        self.high(super().zf)

    def d(self):
        self.high(self.s2)

    def e(self):
        self.high(lambda: self.four(10, False, 1 - self.p["c"]).wait_recv())

    def sent(self):
        for cp in (*self.spread(True), *self.forward(True)):
            cp.wait_send()
        self.four(9, True, self.p["c"]).wait_send()
        self.low(lambda: self.across(True).wait_send())

        def other():
            for cp in (*self.spread(False), *self.forward(False)):
                cp.wait_send()
            self.four(10, False, self.p["c"]).wait_send()

        self.high(other)


def dot(a, b):
    return jnp.dot(a, b, preferred_element_type=F32)


def dot_t(a, b, precision=None):
    return lax.dot_general(
        a, b, (((1,), (1,)), ((), ())), preferred_element_type=F32, precision=precision
    )


def window_kernel(
    x_ref, w_ref, rate_w_ref, near_ref, base_ref, bias_ref, rate_ref, skip_ref,
    teacher_ref, student_ref,
    wkv, wq, xp, own_kv, own_q, qsend, qrecv, kvsend, kvrecv, rawsend, rawrecv,
    kall, vall, stall, sx, rq, ct, vrow, brow, contrib, inner, acc, top,
    wssem, wrsem, gssem, grsem, kssem, krsem, xssem, xrsem, xsem,
):
    p = places()
    g, s, zh, c, zy = p["g"], p["s"], p["zh"], p["c"], p["zy"]
    w = {}
    for n, name in enumerate(KINDS):
        buf = wkv.at[n] if n < 2 else wq.at[n - 2]
        w[name] = Gather(buf, wssem.at[n], wrsem.at[n], p, 64)
    kept = {
        name: Earlier(buf, kssem.at[n], krsem.at[n], p, half)
        for n, (name, buf, half) in enumerate((("k", kall, 64), ("v", vall, 64), ("s", stall, 128)))
    }

    def place(name):
        if name in "kv":
            n = "kv".index(name)
            for k in range(2):
                first = 1024 + n * 128
                wkv[n, c, zy, :, k * 128 : k * 128 + 128] = w_ref[:, k, first : first + 128]
            return
        n = int(name[1])
        for d in range(4):
            first = d % 2 * 512 + n * 128
            wq[n, c, zy, :, d * 128 : d * 128 + 128] = w_ref[:, d // 2, first : first + 128]

    def tile(source, target, k, d):
        return pltpu.make_async_remote_copy(
            src_ref=source, dst_ref=target, send_sem=gssem.at[k, d], recv_sem=grsem.at[k, d],
            device_id=p["G"][d], device_id_type=MESH,
        )

    def raw_tile(d):
        return tile(rawsend.at[lax.rem(g + d + 1, 4)], rawrecv.at[d], len(KINDS), d)

    def tiles(name):
        k = KINDS.index(name)
        if k < 2:
            return [
                tile(kvsend.at[k, lax.rem(g + d + 1, 4) // 2], kvrecv.at[k, d], k, d) for d in range(3)
            ]
        return [
            tile(qsend.at[k - 2, lax.rem(g + d + 1, 4)], qrecv.at[k - 2, d], k, d) for d in range(3)
        ]

    def x_copies():
        for core in range(2):
            for at in range(8):
                src = (at * 2 + core) * 128
                yield pltpu.make_async_copy(
                    x_ref.at[:, src : src + 128], xp.at[core, :, at * 128 : at * 128 + 128],
                    xsem.at[core * 8 + at],
                )

    def arrange():
        for cp in x_copies():
            cp.wait()

    def send_raw():
        raw = 0.0
        for core in range(2):
            parts = [rate_w_ref[:, (at * 2 + core) * 128 : (at * 2 + core) * 128 + 128] for at in range(8)]
            raw = raw + dot_t(jnp.concatenate(parts, axis=1), xp[core])
        for d in range(4):
            rawsend[d] = jnp.concatenate([raw[4 * d : 4 * d + 4], raw[4 * d : 4 * d + 4]], axis=0)
        for d in range(3):
            raw_tile(d).start()

    def rotate(u):
        near_c, near_s = near_ref[0], near_ref[1]
        far_c, far_s = base_ref[0, pl.ds(s, 1), :], base_ref[1, pl.ds(s, 1), :]
        lane = lax.broadcasted_iota(jnp.int32, (1, HEAD_DIM), 1)
        sign = jnp.where(lane < HEAD_DIM // 2, -1.0, 1.0)
        cosine = near_c * far_c - near_s * far_s
        sine = (near_s * far_c + near_c * far_s) * sign
        return u * cosine + pltpu.roll(u, HEAD_DIM // 2, 1) * sine

    def multiply(name):
        w[name].e()
        k = KINDS.index(name)
        buf = wkv.at[k] if k < 2 else wq.at[k - 2]
        out = sum(dot(xp[core], buf[core].reshape(1024, buf.shape[-1])) for core in range(2))
        for d in range(buf.shape[-1] // 128):
            part = out[:, d * 128 : d * 128 + 128]
            if k < 2:
                own_kv[k, d] = part
                kvsend[k, d] = part.astype(BF)
            else:
                own_q[k % 2, d] = part
                qsend[k - 2, d] = part.astype(BF)
        for cp in tiles(name):
            cp.start()

    def settle(name):
        k = KINDS.index(name)
        for cp in tiles(name):
            cp.wait_recv()
        got = own_kv[k, g // 2] if k < 2 else own_q[k % 2, g]
        for d in range(3):
            got = got + (kvrecv[k, d] if k < 2 else qrecv[k - 2, d]).astype(F32)
        if name == "k":
            turned = rotate(got).astype(BF)
            for i in range(4):
                kall[c, zy, :, i * 128 : i * 128 + 128] = turned[i * 128 : i * 128 + 128]
            brow[...] = got.astype(BF)
        elif name == "v":
            vall[c, zy] = got.T.astype(BF)
            vrow[...] = got.astype(BF)
        else:
            ct[k - 2] = got.astype(BF)
            rq[k - 2] = (rotate(got) * (SCALE * LOG2E)).astype(BF)

    row = lax.broadcasted_iota(jnp.int32, (8, TOK), 0)

    def per_head(ref):
        out = jnp.full((8, TOK), ref[0], F32)
        for h in range(1, LOCAL_HEADS):
            out = jnp.where(row % LOCAL_HEADS == h, ref[h], out)
        return out

    from_t = lax.broadcasted_iota(jnp.int32, (STRETCH, STRETCH), 0)
    from_s = lax.broadcasted_iota(jnp.int32, (STRETCH, STRETCH), 1)
    causal = from_s <= from_t
    rows_of = [slice(i * STRETCH, (i + 1) * STRETCH) for i in range(2)]

    def decays():
        total = rawsend[g]
        for d in range(3):
            raw_tile(d).wait_recv()
            total = total + rawrecv[d]
        arg = total + per_head(bias_ref)
        step = jnp.maximum(arg, 0.0) + jnp.log1p(jnp.exp(-jnp.abs(arg)))
        decay = -per_head(rate_ref) * step
        lower = causal.astype(F32)
        upper = (from_t <= from_s).astype(F32)
        pieces = []
        for i in range(2):
            part = decay[:, rows_of[i]]
            cum_row = jnp.dot(part, upper, preferred_element_type=F32, precision=lax.Precision.HIGHEST)
            cum_col = dot_t(lower, part, lax.Precision.HIGHEST)
            end = jnp.exp(jnp.broadcast_to(cum_row[:, STRETCH - 1 :], (8, HEAD_DIM)))
            pieces.append((cum_row, cum_col, step[:, rows_of[i]], end))
        return pieces

    def swap():
        return pltpu.make_async_remote_copy(
            src_ref=sx.at[c], dst_ref=sx.at[c], send_sem=xssem, recv_sem=xrsem,
            device_id=p["S"], device_id_type=MESH,
        )

    def swapped():
        return pltpu.make_async_remote_copy(
            src_ref=sx.at[1 - c], dst_ref=sx.at[1 - c], send_sem=xssem, recv_sem=xrsem,
            device_id=p["S"], device_id_type=MESH,
        )

    def split(value):
        high = value.astype(BF)
        return jnp.concatenate([high, (value - high.astype(F32)).astype(BF)], axis=0)

    def local_state(pieces):
        for i in range(2):
            cum_row, _, rate, _ = pieces[i]
            turned = brow[rows_of[i]].astype(F32).T
            weight = jnp.exp(cum_row[:, STRETCH - 1 :] - cum_row) * rate
            for h in range(LOCAL_HEADS):
                contrib[i, h] = dot((turned * weight[h : h + 1]).astype(BF), vrow[rows_of[i]])
        for h in range(LOCAL_HEADS):
            local = pieces[1][3][h : h + 1] * contrib[0, h] + contrib[1, h]
            sx[c, h * 128 : h * 128 + 128] = local.astype(BF)
        sx[c, 512:528] = split(pieces[0][3] * pieces[1][3])
        swap().start()

    def whole(ref, first):
        both = ref[first : first + 16].astype(F32)
        return both[:8] + both[8:]

    def chip_state():
        swapped().wait_recv()
        first, second = whole(sx.at[0], 512), whole(sx.at[1], 512)
        for k in range(2):
            at = pl.ds(pl.multiple_of(c * 256 + k * 128, 128), 128)
            decay = jnp.where(c == 0, second[k : k + 1], second[k + 2 : k + 3])
            both = decay * sx[0, at].astype(F32) + sx[1, at].astype(F32)
            stall[c, zy, k * 128 : k * 128 + 128] = both.astype(BF)
        stall[c, zy, 256:272] = split(first * second)

    def inside(pieces, h):
        for i in range(2):
            cum_row, cum_col, rate, _ = pieces[i]
            gram = dot_t(ct[h, rows_of[i]], brow[rows_of[i]])
            diff = cum_col[:, h : h + 1] - cum_row[h : h + 1]
            mix = jnp.exp(jnp.where(causal, diff, FAR_BELOW)) * (rate[h : h + 1] * SCALE) * gram
            value = vrow[rows_of[i]]
            inner[h, rows_of[i]] = dot(mix.astype(BF), value) + skip_ref[h] * value.astype(F32)

    def arriving():
        def advance(d, carried):
            blocks = [stall.at[k, d] for k in range(2)]
            total = whole(blocks[0], 256)
            return tuple(
                total[h : h + 1] * carried[h]
                + blocks[h // 2][h % 2 * 128 : h % 2 * 128 + 128].astype(F32)
                for h in range(LOCAL_HEADS)
            )

        zero = jnp.zeros((HEAD_DIM, HEAD_DIM), F32)
        carried = lax.fori_loop(0, zy, advance, (zero,) * LOCAL_HEADS)
        first = whole(sx.at[0], 512)
        return [
            jnp.where(
                c == 0, carried[h],
                first[h : h + 1] * carried[h] + sx[0, h * 128 : h * 128 + 128].astype(F32),
            )
            for h in range(LOCAL_HEADS)
        ]

    def student(pieces, incoming, h):
        for i in range(2):
            reach = jnp.exp(pieces[i][1]) * SCALE
            state = incoming[h] if i == 0 else pieces[0][3][h : h + 1] * incoming[h] + contrib[0, h]
            carried = dot(ct[h, rows_of[i]], state.astype(BF))
            out = inner[h, rows_of[i]] + reach[:, h : h + 1] * carried
            student_ref[rows_of[i], h * 128 : h * 128 + 128] = out.astype(BF)

    ones = jnp.ones((16, TOK), BF)

    def absorb(blocks, heads, diagonal=False):
        todo = [(b, h, i) for b in range(len(blocks)) for h in heads for i in range(TOK // HALF)]

        def scores(n):
            b, h, i = todo[n]
            keys = kall[(*blocks[b],)]
            keys = jnp.concatenate([keys[:, k * 128 : k * 128 + 128] for k in range(4)], axis=0)
            out = dot_t(keys, rq[h, i * HALF : i * HALF + HALF])
            if diagonal:
                at_u = lax.broadcasted_iota(jnp.int32, out.shape, 0)
                at_t = lax.broadcasted_iota(jnp.int32, out.shape, 1) + i * HALF
                out = jnp.where(at_u <= at_t, out, FAR_BELOW)
            return out

        found = {n: scores(n) for n in range(min(2, len(todo)))}
        ready = None
        for n in range(len(todo) + 1):
            now = None
            if n + 2 < len(todo):
                found[n + 2] = scores(n + 2)
            if n < len(todo):
                b, h, i = todo[n]
                cols = slice(i * HALF, i * HALF + HALF)
                score = found.pop(n)
                high = jnp.max(score, axis=0, keepdims=True)
                if diagonal:
                    peak, shrink = high, None
                else:
                    before = top[h, 0:1, cols]
                    peak = jnp.maximum(before, high)
                    shrink = jnp.exp2(before - peak)
                now = (b, h, cols, jnp.exp2(score - peak).astype(BF), shrink)
                top[h, 0:1, cols] = peak
            if ready is not None:
                b, h, cols, weights, shrink = ready
                mixed = dot(jnp.concatenate([vall[(*blocks[b],)], ones], axis=0), weights)
                acc[h, :, cols] = mixed if diagonal else mixed + acc[h, :, cols] * shrink
            ready = now

    def own_part(heads, part):
        if part == 0:
            absorb([(c, zy)], heads, True)
            return
        if part == 1:
            pl.when(c == 1)(lambda: absorb([(0, zy)], heads))
            return

        def visit(j, carry):
            absorb([(0, j), (1, j)], heads)
            return carry

        lax.fori_loop(zh * 4, zy, visit, 0)

    def low_part(heads, part):
        first = part * 2

        def both():
            if len(heads) > 1:
                absorb([(0, first), (1, first)], heads)
                absorb([(0, first + 1), (1, first + 1)], heads)
            else:
                absorb([(k % 2, first + k // 2) for k in range(4)], heads)

        pl.when(zh == 1)(both)

    def teacher(h):
        done = acc[h]
        out = (done[:128] / done[128:129]).T
        teacher_ref[:, h * 128 : h * 128 + 128] = out.astype(BF)

    for cp in x_copies():
        cp.start()
    place("k")
    enter(["R", "L", "Z", "S", "G"], p)
    w["k"].ay()
    w["k"].az()
    arrange()
    send_raw()
    place("v")
    w["v"].ay()
    place("q0")
    w["q0"].ay()
    w["k"].f()
    place("q3")
    w["v"].az()
    w["v"].f()
    w["q3"].ay()
    w["k"].zs()
    w["q0"].az()
    w["k"].s1()
    w["q0"].f()
    w["v"].s1()
    w["v"].zs()
    w["k"].zf()
    w["q3"].f()
    place("q1")
    w["q1"].ay()
    w["q1"].az()
    w["q0"].s1()
    w["v"].zf()
    w["k"].s2()
    w["q3"].s1()
    place("q2")
    w["q0"].zs()
    w["q2"].az()
    w["q2"].ay()
    multiply("k")
    pieces = decays()
    w["v"].s2()
    w["q0"].zf()
    w["q1"].zs()
    w["q3"].az()
    w["q1"].f()
    multiply("v")
    w["q2"].f()
    w["q0"].s2()
    w["q1"].zf()
    w["q2"].zs()
    w["q1"].s1()
    settle("k")
    kept["k"].a()
    multiply("q0")
    w["q2"].s1()
    w["q1"].s2()
    settle("v")
    local_state(pieces)
    w["q2"].zf()
    w["q3"].zs()
    kept["v"].a()
    multiply("q1")
    w["q2"].s2()
    w["q3"].zf()
    kept["k"].b()
    settle("q0")
    multiply("q2")
    kept["v"].b()
    kept["k"].zs()
    chip_state()
    kept["s"].a()
    kept["v"].zs()
    inside(pieces, 0)
    w["q3"].s2()
    kept["k"].c()
    kept["v"].c()
    settle("q1")
    own_part([0, 1], 0)
    multiply("q3")
    kept["k"].near()
    kept["s"].zs()
    inside(pieces, 1)
    kept["k"].zf()
    kept["v"].near()
    own_part([0, 1], 2)
    kept["v"].zf()
    kept["s"].b()
    settle("q2")
    inside(pieces, 2)
    own_part([2], 0)
    own_part([2], 1)
    kept["k"].d()
    kept["s"].zf()
    own_part([2], 2)
    own_part([0, 1], 1)
    kept["v"].d()
    kept["s"].d()
    settle("q3")
    own_part([3], 0)
    inside(pieces, 3)
    kept["k"].e()
    kept["s"].c()
    own_part([3], 2)
    kept["v"].e()
    low_part([3], 0)
    low_part([0, 1], 1)
    low_part([2], 0)
    low_part([0, 1], 0)
    teacher(0)
    kept["s"].near()
    kept["s"].e()
    own_part([3], 1)
    incoming = arriving()
    student(pieces, incoming, 3)
    student(pieces, incoming, 2)
    low_part([2], 1)
    student(pieces, incoming, 1)
    low_part([3], 1)
    teacher(2)
    student(pieces, incoming, 0)
    teacher(3)
    teacher(1)
    for name in KINDS:
        w[name].sent()
        for cp in tiles(name):
            cp.wait_send()
    for d in range(3):
        raw_tile(d).wait_send()
    for name in kept:
        kept[name].sent()
    swap().wait_send()


def tables():
    half = HEAD_DIM // 2
    freq = ROPE_BASE ** (-2.0 * np.arange(half) / HEAD_DIM)
    freq = np.concatenate([freq, freq])
    near = np.arange(TOK)[:, None] * freq[None]
    base = (np.arange(16) * TOK)[:, None] * freq[None]
    return (
        np.stack([np.cos(near), np.sin(near)]).astype(np.float32),
        np.stack([np.cos(base), np.sin(base)]).astype(np.float32),
    )


def hand_over_kernel(teacher_ref, student_ref, teacher_out, student_out):
    teacher_out[...] = teacher_ref[...]
    student_out[...] = student_ref[...]


def body(layer_input, attn_weight, rate_weight, rate_bias, decay_rate, skip_gain):
    vmem = pl.BlockSpec(memory_space=pltpu.VMEM)
    smem = pl.BlockSpec(memory_space=pltpu.SMEM)
    dma = pltpu.SemaphoreType.DMA
    near, base = tables()
    heads = (LOCAL_HEADS, TOK, HEAD_DIM)
    results = pl.pallas_call(
        window_kernel,
        name="window",
        out_shape=(
            jax.ShapeDtypeStruct((TOK, 512), BF),
            jax.ShapeDtypeStruct((TOK, 512), BF),
        ),
        in_specs=[pl.BlockSpec(memory_space=pl.ANY)] + [vmem] * 4 + [smem] * 3,
        out_specs=(vmem, vmem),
        scratch_shapes=[
            pltpu.VMEM((2, 2, 8, 128, 256), BF),
            pltpu.VMEM((4, 2, 8, 128, 512), BF),
            pltpu.VMEM((2, TOK, 1024), BF),
            pltpu.VMEM((2, 2, TOK, 128), F32),
            pltpu.VMEM((2, 4, TOK, 128), F32),
            pltpu.VMEM((4, 4, TOK, 128), BF),
            pltpu.VMEM((4, 3, TOK, 128), BF),
            pltpu.VMEM((2, 2, TOK, 128), BF),
            pltpu.VMEM((2, 3, TOK, 128), BF),
            pltpu.VMEM((4, 8, TOK), F32),
            pltpu.VMEM((3, 8, TOK), F32),
            pltpu.VMEM((2, 8, 128, TOK), BF),
            pltpu.VMEM((2, 8, 128, TOK), BF),
            pltpu.VMEM((2, 8, 272, 128), BF),
            pltpu.VMEM((2, 528, 128), BF),
            pltpu.VMEM(heads, BF),
            pltpu.VMEM(heads, BF),
            pltpu.VMEM((TOK, HEAD_DIM), BF),
            pltpu.VMEM((TOK, HEAD_DIM), BF),
            pltpu.VMEM((2, LOCAL_HEADS, HEAD_DIM, HEAD_DIM), F32),
            pltpu.VMEM(heads, F32),
            pltpu.VMEM((LOCAL_HEADS, 144, TOK), F32),
            pltpu.VMEM((LOCAL_HEADS, 8, TOK), F32),
            dma((len(KINDS), COPIES)),
            dma((len(KINDS), COPIES)),
            dma((len(KINDS) + 1, 3)),
            dma((len(KINDS) + 1, 3)),
            dma((3, COPIES)),
            dma((3, COPIES)),
            dma,
            dma,
            dma((16,)),
        ],
        compiler_params=pltpu.CompilerParams(
            collective_id=0, has_side_effects=True, vmem_limit_bytes=58 * 2**20
        ),
    )(
        layer_input, attn_weight, rate_weight.T, jnp.asarray(near),
        jnp.asarray(base), rate_bias, decay_rate, skip_gain,
    )
    half = pl.BlockSpec((TOK // 2, 512), lambda i: (i, 0))
    return pl.pallas_call(
        hand_over_kernel,
        name="hand_over",
        grid=(2,),
        out_shape=(jax.ShapeDtypeStruct((TOK, 512), BF),) * 2,
        in_specs=[half] * 2,
        out_specs=(half,) * 2,
    )(*results)


def solution(mesh):
    placed = (
        P("seq", "grp"),
        P(("grp", "seq"), "mdl", None),
        P("grp", "mdl"),
        P(("mdl", "grp")),
        P(("mdl", "grp")),
        P(("mdl", "grp")),
    )
    return jax.shard_map(
        body,
        mesh=mesh,
        in_specs=placed,
        out_specs=(P("seq", ("mdl", "grp")), P("seq", ("mdl", "grp"))),
        check_vma=False,
    )
```

```python
import functools
import math

import jax
import jax.numpy as jnp
import numpy as np
from jax import lax
from jax.experimental import pallas as pl
from jax.experimental.pallas import tpu as pltpu
from jax.sharding import PartitionSpec as P

HEAD_DIM = 128
STRETCH = 256
ROPE_BASE = 500000.0
FAR_BELOW = -1e30
TOK = 512
LOCAL_HEADS = 4
KINDS = ("k", "v", "q0", "q1", "q2", "q3")
COPIES = 11
HALF = 256
SCALE = HEAD_DIM**-0.5
LOG2E = math.log2(math.e)
MESH = pl.DeviceIdType.MESH
BF = jnp.bfloat16
F32 = jnp.float32


def places():
    g, s, m = lax.axis_index("grp"), lax.axis_index("seq"), lax.axis_index("mdl")
    zh, y, c = s // 8, (s // 2) % 4, s % 2

    def seq(zh, y, c):
        return zh * 8 + y * 2 + c

    up, down, far = lax.rem(y + 1, 4), lax.rem(y + 3, 4), lax.rem(y + 2, 4)
    return {
        "g": g, "s": s, "zh": zh, "y": y, "c": c,
        "zy": zh * 4 + y,
        "up": up, "down": down, "far": far,
        "R": (g, seq(zh, up, c), m),
        "L": (g, seq(zh, down, c), m),
        "Z": (g, seq(1 - zh, y, c), m),
        "S": (g, seq(zh, y, 1 - c), m),
        "G": [(lax.rem(g + d, 4), s, m) for d in (1, 2, 3)],
    }


def enter(names, p):
    bar = pltpu.get_barrier_semaphore()
    targets = []
    for name in names:
        targets += p[name] if name == "G" else [p[name]]
    for dev in targets:
        pl.semaphore_signal(bar, inc=1, device_id=dev, device_id_type=MESH)
    pl.semaphore_wait(bar, len(targets))


class Gather:
    def __init__(self, buf, ssem, rsem, p, half):
        self.buf, self.ssem, self.rsem, self.p = buf, ssem, rsem, p
        self.rows, self.half = buf.shape[-2], half

    def remote(self, k, ref, dev):
        return pltpu.make_async_remote_copy(
            src_ref=ref, dst_ref=ref, send_sem=self.ssem.at[k], recv_sem=self.rsem.at[k],
            device_id=dev, device_id_type=MESH,
        )

    def copy(self, k, dev, zy, first=None, count=None):
        c = self.p["c"]
        ref = self.buf.at[c, zy] if first is None else self.buf.at[c, zy, pl.ds(first, count)]
        return self.remote(k, ref, dev)

    def four(self, k, own, core):
        return self.remote(k, self.buf.at[core, pl.ds(self.base(own), 4)], self.p["S"])

    def base(self, own):
        return (self.p["zh"] if own else 1 - self.p["zh"]) * 4

    def spread(self, own):
        p, k = self.p, 0 if own else 5
        at = self.base(own) + p["y"]
        return self.copy(k, p["R"], at), self.copy(k + 1, p["L"], at)

    def arrive(self, own):
        p, k = self.p, 0 if own else 5
        return (
            self.copy(k, p["R"], self.base(own) + p["down"]),
            self.copy(k + 1, p["L"], self.base(own) + p["up"]),
        )

    def pair(self, own, left, right):
        p, k = self.p, 2 if own else 7
        return (
            self.copy(k, p["R"], self.base(own) + left, 0, self.half),
            self.copy(k + 1, p["L"], self.base(own) + right, self.half, self.rows - self.half),
        )

    def forward(self, own):
        return self.pair(own, self.p["down"], self.p["up"])

    def halves(self, own):
        return self.pair(own, self.p["far"], self.p["far"])

    def across(self, own):
        return self.copy(4, self.p["Z"], self.base(own) + self.p["y"])

    def ay(self):
        for cp in self.spread(True):
            cp.start()

    def az(self):
        self.across(True).start()

    def pass_on(self, own):
        for got, on in zip(self.arrive(own), self.forward(own)):
            got.wait_recv()
            on.start()

    def f(self):
        self.pass_on(True)

    def zs(self):
        self.across(False).wait_recv()
        for cp in self.spread(False):
            cp.start()

    def finish(self, own):
        for cp in self.halves(own):
            cp.wait_recv()
        self.four(9 if own else 10, own, self.p["c"]).start()

    def s1(self):
        self.finish(True)

    def zf(self):
        self.pass_on(False)

    def s2(self):
        self.finish(False)

    def e(self):
        for own in (True, False):
            self.four(9 if own else 10, own, 1 - self.p["c"]).wait_recv()

    def sent(self):
        for own in (True, False):
            for cp in (*self.spread(own), *self.forward(own)):
                cp.wait_send()
            self.four(9 if own else 10, own, self.p["c"]).wait_send()
        self.across(True).wait_send()


class Earlier(Gather):
    def low(self, f):
        pl.when(self.p["zh"] == 0)(f)

    def high(self, f):
        pl.when(self.p["zh"] == 1)(f)

    def a(self):
        self.low(self.az)
        self.ay()

    def b(self):
        self.f()

    def c(self):
        self.s1()

    def near(self):
        self.four(9, True, 1 - self.p["c"]).wait_recv()

    def zs(self):
        self.high(super().zs)

    def zf(self):
        self.high(super().zf)

    def d(self):
        self.high(self.s2)

    def e(self):
        self.high(lambda: self.four(10, False, 1 - self.p["c"]).wait_recv())

    def sent(self):
        for cp in (*self.spread(True), *self.forward(True)):
            cp.wait_send()
        self.four(9, True, self.p["c"]).wait_send()
        self.low(lambda: self.across(True).wait_send())

        def other():
            for cp in (*self.spread(False), *self.forward(False)):
                cp.wait_send()
            self.four(10, False, self.p["c"]).wait_send()

        self.high(other)


def dot(a, b):
    return jnp.dot(a, b, preferred_element_type=F32)


def dot_t(a, b, precision=None):
    return lax.dot_general(
        a, b, (((1,), (1,)), ((), ())), preferred_element_type=F32, precision=precision
    )


def window_kernel(
    x_ref, w_ref, rate_w_ref, near_ref, base_ref, bias_ref, rate_ref, skip_ref,
    teacher_ref, student_ref,
    wkv, wq, xp, own_kv, own_q, qsend, qrecv, kvsend, kvrecv, rawsend, rawrecv,
    kall, vall, stall, sx, rq, ct, vrow, brow, contrib, inner, acc, top,
    wssem, wrsem, gssem, grsem, kssem, krsem, xssem, xrsem, xsem,
):
    p = places()
    g, s, zh, c, zy = p["g"], p["s"], p["zh"], p["c"], p["zy"]
    w = {}
    for n, name in enumerate(KINDS):
        buf = wkv.at[n] if n < 2 else wq.at[n - 2]
        w[name] = Gather(buf, wssem.at[n], wrsem.at[n], p, 64)
    kept = {
        name: Earlier(buf, kssem.at[n], krsem.at[n], p, half)
        for n, (name, buf, half) in enumerate((("k", kall, 64), ("v", vall, 64), ("s", stall, 128)))
    }

    def place(name):
        if name in "kv":
            n = "kv".index(name)
            for k in range(2):
                first = 1024 + n * 128
                wkv[n, c, zy, :, k * 128 : k * 128 + 128] = w_ref[:, k, first : first + 128]
            return
        n = int(name[1])
        for d in range(4):
            first = d % 2 * 512 + n * 128
            wq[n, c, zy, :, d * 128 : d * 128 + 128] = w_ref[:, d // 2, first : first + 128]

    def tile(source, target, k, d):
        return pltpu.make_async_remote_copy(
            src_ref=source, dst_ref=target, send_sem=gssem.at[k, d], recv_sem=grsem.at[k, d],
            device_id=p["G"][d], device_id_type=MESH,
        )

    def raw_tile(d):
        return tile(rawsend.at[lax.rem(g + d + 1, 4)], rawrecv.at[d], len(KINDS), d)

    def tiles(name):
        k = KINDS.index(name)
        if k < 2:
            return [
                tile(kvsend.at[k, lax.rem(g + d + 1, 4) // 2], kvrecv.at[k, d], k, d) for d in range(3)
            ]
        return [
            tile(qsend.at[k - 2, lax.rem(g + d + 1, 4)], qrecv.at[k - 2, d], k, d) for d in range(3)
        ]

    def x_copies():
        for core in range(2):
            for at in range(8):
                src = (at * 2 + core) * 128
                yield pltpu.make_async_copy(
                    x_ref.at[:, src : src + 128], xp.at[core, :, at * 128 : at * 128 + 128],
                    xsem.at[core * 8 + at],
                )

    def arrange():
        for cp in x_copies():
            cp.wait()

    def send_raw():
        raw = 0.0
        for core in range(2):
            parts = [rate_w_ref[:, (at * 2 + core) * 128 : (at * 2 + core) * 128 + 128] for at in range(8)]
            raw = raw + dot_t(jnp.concatenate(parts, axis=1), xp[core])
        for d in range(4):
            rawsend[d] = jnp.concatenate([raw[4 * d : 4 * d + 4], raw[4 * d : 4 * d + 4]], axis=0)
        for d in range(3):
            raw_tile(d).start()

    def rotate(u):
        near_c, near_s = near_ref[0], near_ref[1]
        far_c, far_s = base_ref[0, pl.ds(s, 1), :], base_ref[1, pl.ds(s, 1), :]
        lane = lax.broadcasted_iota(jnp.int32, (1, HEAD_DIM), 1)
        sign = jnp.where(lane < HEAD_DIM // 2, -1.0, 1.0)
        cosine = near_c * far_c - near_s * far_s
        sine = (near_s * far_c + near_c * far_s) * sign
        return u * cosine + pltpu.roll(u, HEAD_DIM // 2, 1) * sine

    def multiply(name):
        w[name].e()
        k = KINDS.index(name)
        buf = wkv.at[k] if k < 2 else wq.at[k - 2]
        out = sum(dot(xp[core], buf[core].reshape(1024, buf.shape[-1])) for core in range(2))
        for d in range(buf.shape[-1] // 128):
            part = out[:, d * 128 : d * 128 + 128]
            if k < 2:
                own_kv[k, d] = part
                kvsend[k, d] = part.astype(BF)
            else:
                own_q[k % 2, d] = part
                qsend[k - 2, d] = part.astype(BF)
        for cp in tiles(name):
            cp.start()

    def settle(name):
        k = KINDS.index(name)
        for cp in tiles(name):
            cp.wait_recv()
        got = own_kv[k, g // 2] if k < 2 else own_q[k % 2, g]
        for d in range(3):
            got = got + (kvrecv[k, d] if k < 2 else qrecv[k - 2, d]).astype(F32)
        if name == "k":
            turned = rotate(got).astype(BF)
            for i in range(4):
                kall[c, zy, :, i * 128 : i * 128 + 128] = turned[i * 128 : i * 128 + 128]
            brow[...] = got.astype(BF)
        elif name == "v":
            vall[c, zy] = got.T.astype(BF)
            vrow[...] = got.astype(BF)
        else:
            ct[k - 2] = got.astype(BF)
            rq[k - 2] = (rotate(got) * (SCALE * LOG2E)).astype(BF)

    row = lax.broadcasted_iota(jnp.int32, (8, TOK), 0)

    def per_head(ref):
        out = jnp.full((8, TOK), ref[0], F32)
        for h in range(1, LOCAL_HEADS):
            out = jnp.where(row % LOCAL_HEADS == h, ref[h], out)
        return out

    from_t = lax.broadcasted_iota(jnp.int32, (STRETCH, STRETCH), 0)
    from_s = lax.broadcasted_iota(jnp.int32, (STRETCH, STRETCH), 1)
    causal = from_s <= from_t
    rows_of = [slice(i * STRETCH, (i + 1) * STRETCH) for i in range(2)]

    def decays():
        total = rawsend[g]
        for d in range(3):
            raw_tile(d).wait_recv()
            total = total + rawrecv[d]
        arg = total + per_head(bias_ref)
        step = jnp.maximum(arg, 0.0) + jnp.log1p(jnp.exp(-jnp.abs(arg)))
        decay = -per_head(rate_ref) * step
        lower = causal.astype(F32)
        upper = (from_t <= from_s).astype(F32)
        pieces = []
        for i in range(2):
            part = decay[:, rows_of[i]]
            cum_row = jnp.dot(part, upper, preferred_element_type=F32, precision=lax.Precision.HIGHEST)
            cum_col = dot_t(lower, part, lax.Precision.HIGHEST)
            end = jnp.exp(jnp.broadcast_to(cum_row[:, STRETCH - 1 :], (8, HEAD_DIM)))
            pieces.append((cum_row, cum_col, step[:, rows_of[i]], end))
        return pieces

    def swap():
        return pltpu.make_async_remote_copy(
            src_ref=sx.at[c], dst_ref=sx.at[c], send_sem=xssem, recv_sem=xrsem,
            device_id=p["S"], device_id_type=MESH,
        )

    def swapped():
        return pltpu.make_async_remote_copy(
            src_ref=sx.at[1 - c], dst_ref=sx.at[1 - c], send_sem=xssem, recv_sem=xrsem,
            device_id=p["S"], device_id_type=MESH,
        )

    def split(value):
        high = value.astype(BF)
        return jnp.concatenate([high, (value - high.astype(F32)).astype(BF)], axis=0)

    def local_state(pieces):
        for i in range(2):
            cum_row, _, rate, _ = pieces[i]
            turned = brow[rows_of[i]].astype(F32).T
            weight = jnp.exp(cum_row[:, STRETCH - 1 :] - cum_row) * rate
            for h in range(LOCAL_HEADS):
                contrib[i, h] = dot((turned * weight[h : h + 1]).astype(BF), vrow[rows_of[i]])
        for h in range(LOCAL_HEADS):
            local = pieces[1][3][h : h + 1] * contrib[0, h] + contrib[1, h]
            sx[c, h * 128 : h * 128 + 128] = local.astype(BF)
        sx[c, 512:528] = split(pieces[0][3] * pieces[1][3])
        swap().start()

    def whole(ref, first):
        both = ref[first : first + 16].astype(F32)
        return both[:8] + both[8:]

    def chip_state():
        swapped().wait_recv()
        first, second = whole(sx.at[0], 512), whole(sx.at[1], 512)
        for k in range(2):
            at = pl.ds(pl.multiple_of(c * 256 + k * 128, 128), 128)
            decay = jnp.where(c == 0, second[k : k + 1], second[k + 2 : k + 3])
            both = decay * sx[0, at].astype(F32) + sx[1, at].astype(F32)
            stall[c, zy, k * 128 : k * 128 + 128] = both.astype(BF)
        stall[c, zy, 256:272] = split(first * second)

    def inside(pieces, h):
        for i in range(2):
            cum_row, cum_col, rate, _ = pieces[i]
            gram = dot_t(ct[h, rows_of[i]], brow[rows_of[i]])
            diff = cum_col[:, h : h + 1] - cum_row[h : h + 1]
            mix = jnp.exp(jnp.where(causal, diff, FAR_BELOW)) * (rate[h : h + 1] * SCALE) * gram
            value = vrow[rows_of[i]]
            inner[h, rows_of[i]] = dot(mix.astype(BF), value) + skip_ref[h] * value.astype(F32)

    def arriving():
        def advance(d, carried):
            blocks = [stall.at[k, d] for k in range(2)]
            total = whole(blocks[0], 256)
            return tuple(
                total[h : h + 1] * carried[h]
                + blocks[h // 2][h % 2 * 128 : h % 2 * 128 + 128].astype(F32)
                for h in range(LOCAL_HEADS)
            )

        zero = jnp.zeros((HEAD_DIM, HEAD_DIM), F32)
        carried = lax.fori_loop(0, zy, advance, (zero,) * LOCAL_HEADS)
        first = whole(sx.at[0], 512)
        return [
            jnp.where(
                c == 0, carried[h],
                first[h : h + 1] * carried[h] + sx[0, h * 128 : h * 128 + 128].astype(F32),
            )
            for h in range(LOCAL_HEADS)
        ]

    def student(pieces, incoming, h):
        for i in range(2):
            reach = jnp.exp(pieces[i][1]) * SCALE
            state = incoming[h] if i == 0 else pieces[0][3][h : h + 1] * incoming[h] + contrib[0, h]
            carried = dot(ct[h, rows_of[i]], state.astype(BF))
            out = inner[h, rows_of[i]] + reach[:, h : h + 1] * carried
            student_ref[rows_of[i], h * 128 : h * 128 + 128] = out.astype(BF)

    ones = jnp.ones((16, TOK), BF)

    def absorb(blocks, heads, diagonal=False):
        todo = [(b, h, i) for b in range(len(blocks)) for h in heads for i in range(TOK // HALF)]

        def scores(n):
            b, h, i = todo[n]
            keys = kall[(*blocks[b],)]
            keys = jnp.concatenate([keys[:, k * 128 : k * 128 + 128] for k in range(4)], axis=0)
            out = dot_t(keys, rq[h, i * HALF : i * HALF + HALF])
            if diagonal:
                at_u = lax.broadcasted_iota(jnp.int32, out.shape, 0)
                at_t = lax.broadcasted_iota(jnp.int32, out.shape, 1) + i * HALF
                out = jnp.where(at_u <= at_t, out, FAR_BELOW)
            return out

        found = {n: scores(n) for n in range(min(2, len(todo)))}
        ready = None
        for n in range(len(todo) + 1):
            now = None
            if n + 2 < len(todo):
                found[n + 2] = scores(n + 2)
            if n < len(todo):
                b, h, i = todo[n]
                cols = slice(i * HALF, i * HALF + HALF)
                score = found.pop(n)
                high = jnp.max(score, axis=0, keepdims=True)
                if diagonal:
                    peak, shrink = high, None
                else:
                    before = top[h, 0:1, cols]
                    peak = jnp.maximum(before, high)
                    shrink = jnp.exp2(before - peak)
                now = (b, h, cols, jnp.exp2(score - peak).astype(BF), shrink)
                top[h, 0:1, cols] = peak
            if ready is not None:
                b, h, cols, weights, shrink = ready
                mixed = dot(jnp.concatenate([vall[(*blocks[b],)], ones], axis=0), weights)
                acc[h, :, cols] = mixed if diagonal else mixed + acc[h, :, cols] * shrink
            ready = now

    def own_part(heads, part):
        if part == 0:
            absorb([(c, zy)], heads, True)
            return
        if part == 1:
            pl.when(c == 1)(lambda: absorb([(0, zy)], heads))
            return

        if len(heads) > 1:

            def visit(j, carry):
                absorb([(0, j), (1, j)], heads)
                return carry

            lax.fori_loop(zh * 4, zy, visit, 0)
            return
        first, chips = zh * 4, p["y"]
        pl.when(chips >= 2)(lambda: absorb([(k % 2, first + k // 2) for k in range(4)], heads))
        last = zy - 1
        pl.when(chips % 2 == 1)(lambda: absorb([(0, last), (1, last)], heads))

    def low_part(heads, part):
        if len(heads) > 1:
            blocks = [(k % 2, part * 2 + k // 2) for k in range(4)]
        else:
            blocks = [(k % 2, k // 2) for k in range(8)]
        pl.when(zh == 1)(lambda: absorb(blocks, heads))

    def teacher(h):
        done = acc[h]
        out = (done[:128] / done[128:129]).T
        teacher_ref[:, h * 128 : h * 128 + 128] = out.astype(BF)

    for cp in x_copies():
        cp.start()
    place("k")
    enter(["R", "L", "Z", "S", "G"], p)
    w["k"].ay()
    w["k"].az()
    arrange()
    send_raw()
    place("v")
    w["v"].ay()
    place("q0")
    w["q0"].ay()
    w["k"].f()
    place("q3")
    w["v"].az()
    w["v"].f()
    w["q3"].ay()
    w["k"].zs()
    w["q0"].az()
    w["k"].s1()
    w["q0"].f()
    w["v"].s1()
    w["v"].zs()
    w["k"].zf()
    w["q3"].f()
    place("q1")
    w["q1"].ay()
    w["q1"].az()
    w["q0"].s1()
    w["v"].zf()
    w["k"].s2()
    w["q3"].s1()
    place("q2")
    w["q0"].zs()
    w["q2"].az()
    w["q2"].ay()
    multiply("k")
    pieces = decays()
    w["v"].s2()
    w["q0"].zf()
    w["q1"].zs()
    w["q3"].az()
    w["q1"].f()
    multiply("v")
    w["q2"].f()
    w["q0"].s2()
    w["q1"].zf()
    w["q2"].zs()
    w["q1"].s1()
    settle("k")
    kept["k"].a()
    multiply("q0")
    w["q2"].s1()
    w["q1"].s2()
    settle("v")
    local_state(pieces)
    w["q2"].zf()
    w["q3"].zs()
    kept["v"].a()
    multiply("q1")
    w["q2"].s2()
    w["q3"].zf()
    kept["k"].b()
    settle("q0")
    multiply("q2")
    kept["v"].b()
    kept["k"].zs()
    chip_state()
    kept["s"].a()
    kept["v"].zs()
    inside(pieces, 0)
    w["q3"].s2()
    kept["k"].c()
    kept["v"].c()
    settle("q1")
    own_part([0, 1], 0)
    multiply("q3")
    kept["k"].near()
    kept["s"].zs()
    inside(pieces, 1)
    kept["k"].zf()
    kept["v"].near()
    own_part([0, 1], 2)
    kept["v"].zf()
    kept["s"].b()
    settle("q2")
    inside(pieces, 2)
    own_part([2], 0)
    own_part([2], 1)
    kept["k"].d()
    kept["s"].zf()
    own_part([2], 2)
    own_part([0, 1], 1)
    kept["v"].d()
    kept["s"].d()
    settle("q3")
    own_part([3], 0)
    inside(pieces, 3)
    kept["k"].e()
    kept["s"].c()
    own_part([3], 2)
    kept["v"].e()
    low_part([0, 1], 1)
    low_part([0, 1], 0)
    teacher(0)
    kept["s"].near()
    kept["s"].e()
    own_part([3], 1)
    incoming = arriving()
    student(pieces, incoming, 3)
    student(pieces, incoming, 2)
    low_part([2], 1)
    student(pieces, incoming, 1)
    low_part([3], 1)
    teacher(2)
    student(pieces, incoming, 0)
    teacher(3)
    teacher(1)
    for name in KINDS:
        w[name].sent()
        for cp in tiles(name):
            cp.wait_send()
    for d in range(3):
        raw_tile(d).wait_send()
    for name in kept:
        kept[name].sent()
    swap().wait_send()


def tables():
    half = HEAD_DIM // 2
    freq = ROPE_BASE ** (-2.0 * np.arange(half) / HEAD_DIM)
    freq = np.concatenate([freq, freq])
    near = np.arange(TOK)[:, None] * freq[None]
    base = (np.arange(16) * TOK)[:, None] * freq[None]
    return (
        np.stack([np.cos(near), np.sin(near)]).astype(np.float32),
        np.stack([np.cos(base), np.sin(base)]).astype(np.float32),
    )


def hand_over_kernel(teacher_ref, student_ref, teacher_out, student_out):
    teacher_out[...] = teacher_ref[...]
    student_out[...] = student_ref[...]


def body(layer_input, attn_weight, rate_weight, rate_bias, decay_rate, skip_gain):
    vmem = pl.BlockSpec(memory_space=pltpu.VMEM)
    smem = pl.BlockSpec(memory_space=pltpu.SMEM)
    dma = pltpu.SemaphoreType.DMA
    near, base = tables()
    heads = (LOCAL_HEADS, TOK, HEAD_DIM)
    results = pl.pallas_call(
        window_kernel,
        name="window",
        out_shape=(
            jax.ShapeDtypeStruct((TOK, 512), BF),
            jax.ShapeDtypeStruct((TOK, 512), BF),
        ),
        in_specs=[pl.BlockSpec(memory_space=pl.ANY)] + [vmem] * 4 + [smem] * 3,
        out_specs=(vmem, vmem),
        scratch_shapes=[
            pltpu.VMEM((2, 2, 8, 128, 256), BF),
            pltpu.VMEM((4, 2, 8, 128, 512), BF),
            pltpu.VMEM((2, TOK, 1024), BF),
            pltpu.VMEM((2, 2, TOK, 128), F32),
            pltpu.VMEM((2, 4, TOK, 128), F32),
            pltpu.VMEM((4, 4, TOK, 128), BF),
            pltpu.VMEM((4, 3, TOK, 128), BF),
            pltpu.VMEM((2, 2, TOK, 128), BF),
            pltpu.VMEM((2, 3, TOK, 128), BF),
            pltpu.VMEM((4, 8, TOK), F32),
            pltpu.VMEM((3, 8, TOK), F32),
            pltpu.VMEM((2, 8, 128, TOK), BF),
            pltpu.VMEM((2, 8, 128, TOK), BF),
            pltpu.VMEM((2, 8, 272, 128), BF),
            pltpu.VMEM((2, 528, 128), BF),
            pltpu.VMEM(heads, BF),
            pltpu.VMEM(heads, BF),
            pltpu.VMEM((TOK, HEAD_DIM), BF),
            pltpu.VMEM((TOK, HEAD_DIM), BF),
            pltpu.VMEM((2, LOCAL_HEADS, HEAD_DIM, HEAD_DIM), F32),
            pltpu.VMEM(heads, F32),
            pltpu.VMEM((LOCAL_HEADS, 144, TOK), F32),
            pltpu.VMEM((LOCAL_HEADS, 8, TOK), F32),
            dma((len(KINDS), COPIES)),
            dma((len(KINDS), COPIES)),
            dma((len(KINDS) + 1, 3)),
            dma((len(KINDS) + 1, 3)),
            dma((3, COPIES)),
            dma((3, COPIES)),
            dma,
            dma,
            dma((16,)),
        ],
        compiler_params=pltpu.CompilerParams(
            collective_id=0, has_side_effects=True, vmem_limit_bytes=58 * 2**20
        ),
    )(
        layer_input, attn_weight, rate_weight.T, jnp.asarray(near),
        jnp.asarray(base), rate_bias, decay_rate, skip_gain,
    )
    half = pl.BlockSpec((TOK // 2, 512), lambda i: (i, 0))
    return pl.pallas_call(
        hand_over_kernel,
        name="hand_over",
        grid=(2,),
        out_shape=(jax.ShapeDtypeStruct((TOK, 512), BF),) * 2,
        in_specs=[half] * 2,
        out_specs=(half,) * 2,
    )(*results)


def solution(mesh):
    placed = (
        P("seq", "grp"),
        P(("grp", "seq"), "mdl", None),
        P("grp", "mdl"),
        P(("mdl", "grp")),
        P(("mdl", "grp")),
        P(("mdl", "grp")),
    )
    return jax.shard_map(
        body,
        mesh=mesh,
        in_specs=placed,
        out_specs=(P("seq", ("mdl", "grp")), P("seq", ("mdl", "grp"))),
        check_vma=False,
    )
```

```python
import functools
import math

import jax
import jax.numpy as jnp
import numpy as np
from jax import lax
from jax.experimental import pallas as pl
from jax.experimental.pallas import tpu as pltpu
from jax.sharding import PartitionSpec as P

HEAD_DIM = 128
STRETCH = 256
ROPE_BASE = 500000.0
FAR_BELOW = -1e30
TOK = 512
LOCAL_HEADS = 4
KINDS = ("k", "v", "q0", "q1", "q2", "q3")
COPIES = 11
HALF = 256
SCALE = HEAD_DIM**-0.5
LOG2E = math.log2(math.e)
MESH = pl.DeviceIdType.MESH
BF = jnp.bfloat16
F32 = jnp.float32


def places():
    g, s, m = lax.axis_index("grp"), lax.axis_index("seq"), lax.axis_index("mdl")
    zh, y, c = s // 8, (s // 2) % 4, s % 2

    def seq(zh, y, c):
        return zh * 8 + y * 2 + c

    up, down, far = lax.rem(y + 1, 4), lax.rem(y + 3, 4), lax.rem(y + 2, 4)
    return {
        "g": g, "s": s, "zh": zh, "y": y, "c": c,
        "zy": zh * 4 + y,
        "up": up, "down": down, "far": far,
        "R": (g, seq(zh, up, c), m),
        "L": (g, seq(zh, down, c), m),
        "Z": (g, seq(1 - zh, y, c), m),
        "S": (g, seq(zh, y, 1 - c), m),
        "G": [(lax.rem(g + d, 4), s, m) for d in (1, 2, 3)],
    }


def enter(names, p):
    bar = pltpu.get_barrier_semaphore()
    targets = []
    for name in names:
        targets += p[name] if name == "G" else [p[name]]
    for dev in targets:
        pl.semaphore_signal(bar, inc=1, device_id=dev, device_id_type=MESH)
    pl.semaphore_wait(bar, len(targets))


class Gather:
    def __init__(self, buf, ssem, rsem, p, half):
        self.buf, self.ssem, self.rsem, self.p = buf, ssem, rsem, p
        self.rows, self.half = buf.shape[-2], half

    def remote(self, k, ref, dev):
        return pltpu.make_async_remote_copy(
            src_ref=ref, dst_ref=ref, send_sem=self.ssem.at[k], recv_sem=self.rsem.at[k],
            device_id=dev, device_id_type=MESH,
        )

    def copy(self, k, dev, zy, first=None, count=None):
        c = self.p["c"]
        ref = self.buf.at[c, zy] if first is None else self.buf.at[c, zy, pl.ds(first, count)]
        return self.remote(k, ref, dev)

    def four(self, k, own, core):
        return self.remote(k, self.buf.at[core, pl.ds(self.base(own), 4)], self.p["S"])

    def base(self, own):
        return (self.p["zh"] if own else 1 - self.p["zh"]) * 4

    def spread(self, own):
        p, k = self.p, 0 if own else 5
        at = self.base(own) + p["y"]
        return self.copy(k, p["R"], at), self.copy(k + 1, p["L"], at)

    def arrive(self, own):
        p, k = self.p, 0 if own else 5
        return (
            self.copy(k, p["R"], self.base(own) + p["down"]),
            self.copy(k + 1, p["L"], self.base(own) + p["up"]),
        )

    def pair(self, own, left, right):
        p, k = self.p, 2 if own else 7
        return (
            self.copy(k, p["R"], self.base(own) + left, 0, self.half),
            self.copy(k + 1, p["L"], self.base(own) + right, self.half, self.rows - self.half),
        )

    def forward(self, own):
        return self.pair(own, self.p["down"], self.p["up"])

    def halves(self, own):
        return self.pair(own, self.p["far"], self.p["far"])

    def across(self, own):
        return self.copy(4, self.p["Z"], self.base(own) + self.p["y"])

    def ay(self):
        for cp in self.spread(True):
            cp.start()

    def az(self):
        self.across(True).start()

    def pass_on(self, own):
        for got, on in zip(self.arrive(own), self.forward(own)):
            got.wait_recv()
            on.start()

    def f(self):
        self.pass_on(True)

    def zs(self):
        self.across(False).wait_recv()
        for cp in self.spread(False):
            cp.start()

    def finish(self, own):
        for cp in self.halves(own):
            cp.wait_recv()
        self.four(9 if own else 10, own, self.p["c"]).start()

    def s1(self):
        self.finish(True)

    def zf(self):
        self.pass_on(False)

    def s2(self):
        self.finish(False)

    def e(self):
        for own in (True, False):
            self.four(9 if own else 10, own, 1 - self.p["c"]).wait_recv()

    def sent(self):
        for own in (True, False):
            for cp in (*self.spread(own), *self.forward(own)):
                cp.wait_send()
            self.four(9 if own else 10, own, self.p["c"]).wait_send()
        self.across(True).wait_send()


class Earlier(Gather):
    def low(self, f):
        pl.when(self.p["zh"] == 0)(f)

    def high(self, f):
        pl.when(self.p["zh"] == 1)(f)

    def a(self):
        self.low(self.az)
        self.ay()

    def b(self):
        self.f()

    def c(self):
        self.s1()

    def near(self):
        self.four(9, True, 1 - self.p["c"]).wait_recv()

    def zs(self):
        self.high(super().zs)

    def zf(self):
        self.high(super().zf)

    def d(self):
        self.high(self.s2)

    def e(self):
        self.high(lambda: self.four(10, False, 1 - self.p["c"]).wait_recv())

    def sent(self):
        for cp in (*self.spread(True), *self.forward(True)):
            cp.wait_send()
        self.four(9, True, self.p["c"]).wait_send()
        self.low(lambda: self.across(True).wait_send())

        def other():
            for cp in (*self.spread(False), *self.forward(False)):
                cp.wait_send()
            self.four(10, False, self.p["c"]).wait_send()

        self.high(other)


def dot(a, b):
    return jnp.dot(a, b, preferred_element_type=F32)


def dot_t(a, b, precision=None):
    return lax.dot_general(
        a, b, (((1,), (1,)), ((), ())), preferred_element_type=F32, precision=precision
    )


def window_kernel(
    x_ref, w_ref, rate_w_ref, near_ref, base_ref, bias_ref, rate_ref, skip_ref,
    teacher_ref, student_ref,
    wkv, wq, xp, own_kv, own_q, qsend, qrecv, kvsend, kvrecv, rawsend, rawrecv,
    kall, vall, stall, sx, rq, ct, vrow, brow, contrib, inner, acc, top,
    wssem, wrsem, gssem, grsem, kssem, krsem, xssem, xrsem, xsem,
):
    p = places()
    g, s, zh, c, zy = p["g"], p["s"], p["zh"], p["c"], p["zy"]
    w = {}
    for n, name in enumerate(KINDS):
        buf = wkv.at[n] if n < 2 else wq.at[n - 2]
        w[name] = Gather(buf, wssem.at[n], wrsem.at[n], p, 64)
    kept = {
        name: Earlier(buf, kssem.at[n], krsem.at[n], p, half)
        for n, (name, buf, half) in enumerate((("k", kall, 64), ("v", vall, 64), ("s", stall, 128)))
    }

    def place(name):
        if name in "kv":
            n = "kv".index(name)
            for k in range(2):
                first = 1024 + n * 128
                wkv[n, c, zy, :, k * 128 : k * 128 + 128] = w_ref[:, k, first : first + 128]
            return
        n = int(name[1])
        for d in range(4):
            first = d % 2 * 512 + n * 128
            wq[n, c, zy, :, d * 128 : d * 128 + 128] = w_ref[:, d // 2, first : first + 128]

    def tile(source, target, k, d):
        return pltpu.make_async_remote_copy(
            src_ref=source, dst_ref=target, send_sem=gssem.at[k, d], recv_sem=grsem.at[k, d],
            device_id=p["G"][d], device_id_type=MESH,
        )

    def raw_tile(d):
        return tile(rawsend.at[lax.rem(g + d + 1, 4)], rawrecv.at[d], len(KINDS), d)

    def tiles(name):
        k = KINDS.index(name)
        if k < 2:
            return [
                tile(kvsend.at[k, lax.rem(g + d + 1, 4) // 2], kvrecv.at[k, d], k, d) for d in range(3)
            ]
        return [
            tile(qsend.at[k - 2, lax.rem(g + d + 1, 4)], qrecv.at[k - 2, d], k, d) for d in range(3)
        ]

    def x_copies():
        for core in range(2):
            for at in range(8):
                src = (at * 2 + core) * 128
                yield pltpu.make_async_copy(
                    x_ref.at[:, src : src + 128], xp.at[core, :, at * 128 : at * 128 + 128],
                    xsem.at[core * 8 + at],
                )

    def arrange():
        for cp in x_copies():
            cp.wait()

    def send_raw():
        raw = 0.0
        for core in range(2):
            parts = [rate_w_ref[:, (at * 2 + core) * 128 : (at * 2 + core) * 128 + 128] for at in range(8)]
            raw = raw + dot_t(jnp.concatenate(parts, axis=1), xp[core])
        for d in range(4):
            rawsend[d] = jnp.concatenate([raw[4 * d : 4 * d + 4], raw[4 * d : 4 * d + 4]], axis=0)
        for d in range(3):
            raw_tile(d).start()

    def rotate(u):
        near_c, near_s = near_ref[0], near_ref[1]
        far_c, far_s = base_ref[0, pl.ds(s, 1), :], base_ref[1, pl.ds(s, 1), :]
        lane = lax.broadcasted_iota(jnp.int32, (1, HEAD_DIM), 1)
        sign = jnp.where(lane < HEAD_DIM // 2, -1.0, 1.0)
        cosine = near_c * far_c - near_s * far_s
        sine = (near_s * far_c + near_c * far_s) * sign
        return u * cosine + pltpu.roll(u, HEAD_DIM // 2, 1) * sine

    def multiply(name):
        w[name].e()
        k = KINDS.index(name)
        buf = wkv.at[k] if k < 2 else wq.at[k - 2]
        out = sum(dot(xp[core], buf[core].reshape(1024, buf.shape[-1])) for core in range(2))
        for d in range(buf.shape[-1] // 128):
            part = out[:, d * 128 : d * 128 + 128]
            if k < 2:
                own_kv[k, d] = part
                kvsend[k, d] = part.astype(BF)
            else:
                own_q[k % 2, d] = part
                qsend[k - 2, d] = part.astype(BF)
        for cp in tiles(name):
            cp.start()

    def settle(name):
        k = KINDS.index(name)
        for cp in tiles(name):
            cp.wait_recv()
        got = own_kv[k, g // 2] if k < 2 else own_q[k % 2, g]
        for d in range(3):
            got = got + (kvrecv[k, d] if k < 2 else qrecv[k - 2, d]).astype(F32)
        if name == "k":
            turned = rotate(got).astype(BF)
            for i in range(4):
                kall[c, zy, :, i * 128 : i * 128 + 128] = turned[i * 128 : i * 128 + 128]
            brow[...] = got.astype(BF)
        elif name == "v":
            vall[c, zy] = got.T.astype(BF)
            vrow[...] = got.astype(BF)
        else:
            ct[k - 2] = got.astype(BF)
            rq[k - 2] = (rotate(got) * (SCALE * LOG2E)).astype(BF)

    row = lax.broadcasted_iota(jnp.int32, (8, TOK), 0)

    def per_head(ref):
        out = jnp.full((8, TOK), ref[0], F32)
        for h in range(1, LOCAL_HEADS):
            out = jnp.where(row % LOCAL_HEADS == h, ref[h], out)
        return out

    from_t = lax.broadcasted_iota(jnp.int32, (STRETCH, STRETCH), 0)
    from_s = lax.broadcasted_iota(jnp.int32, (STRETCH, STRETCH), 1)
    causal = from_s <= from_t
    rows_of = [slice(i * STRETCH, (i + 1) * STRETCH) for i in range(2)]

    def decays():
        total = rawsend[g]
        for d in range(3):
            raw_tile(d).wait_recv()
            total = total + rawrecv[d]
        arg = total + per_head(bias_ref)
        step = jnp.maximum(arg, 0.0) + jnp.log1p(jnp.exp(-jnp.abs(arg)))
        decay = -per_head(rate_ref) * step
        lower = causal.astype(F32)
        upper = (from_t <= from_s).astype(F32)
        pieces = []
        for i in range(2):
            part = decay[:, rows_of[i]]
            cum_row = jnp.dot(part, upper, preferred_element_type=F32, precision=lax.Precision.HIGHEST)
            cum_col = dot_t(lower, part, lax.Precision.HIGHEST)
            end = jnp.exp(jnp.broadcast_to(cum_row[:, STRETCH - 1 :], (8, HEAD_DIM)))
            pieces.append((cum_row, cum_col, step[:, rows_of[i]], end))
        return pieces

    def swap():
        return pltpu.make_async_remote_copy(
            src_ref=sx.at[c], dst_ref=sx.at[c], send_sem=xssem, recv_sem=xrsem,
            device_id=p["S"], device_id_type=MESH,
        )

    def swapped():
        return pltpu.make_async_remote_copy(
            src_ref=sx.at[1 - c], dst_ref=sx.at[1 - c], send_sem=xssem, recv_sem=xrsem,
            device_id=p["S"], device_id_type=MESH,
        )

    def split(value):
        high = value.astype(BF)
        return jnp.concatenate([high, (value - high.astype(F32)).astype(BF)], axis=0)

    def local_state(pieces):
        for i in range(2):
            cum_row, _, rate, _ = pieces[i]
            turned = brow[rows_of[i]].astype(F32).T
            weight = jnp.exp(cum_row[:, STRETCH - 1 :] - cum_row) * rate
            for h in range(LOCAL_HEADS):
                contrib[i, h] = dot((turned * weight[h : h + 1]).astype(BF), vrow[rows_of[i]])
        for h in range(LOCAL_HEADS):
            local = pieces[1][3][h : h + 1] * contrib[0, h] + contrib[1, h]
            sx[c, h * 128 : h * 128 + 128] = local.astype(BF)
        sx[c, 512:528] = split(pieces[0][3] * pieces[1][3])
        swap().start()

    def whole(ref, first):
        both = ref[first : first + 16].astype(F32)
        return both[:8] + both[8:]

    def chip_state():
        swapped().wait_recv()
        first, second = whole(sx.at[0], 512), whole(sx.at[1], 512)
        for k in range(2):
            at = pl.ds(pl.multiple_of(c * 256 + k * 128, 128), 128)
            decay = jnp.where(c == 0, second[k : k + 1], second[k + 2 : k + 3])
            both = decay * sx[0, at].astype(F32) + sx[1, at].astype(F32)
            stall[c, zy, k * 128 : k * 128 + 128] = both.astype(BF)
        stall[c, zy, 256:272] = split(first * second)

    def inside(pieces, h):
        for i in range(2):
            cum_row, cum_col, rate, _ = pieces[i]
            gram = dot_t(ct[h, rows_of[i]], brow[rows_of[i]])
            diff = cum_col[:, h : h + 1] - cum_row[h : h + 1]
            mix = jnp.exp(jnp.where(causal, diff, FAR_BELOW)) * (rate[h : h + 1] * SCALE) * gram
            value = vrow[rows_of[i]]
            inner[h, rows_of[i]] = dot(mix.astype(BF), value) + skip_ref[h] * value.astype(F32)

    def arriving():
        def advance(d, carried):
            blocks = [stall.at[k, d] for k in range(2)]
            total = whole(blocks[0], 256)
            return tuple(
                total[h : h + 1] * carried[h]
                + blocks[h // 2][h % 2 * 128 : h % 2 * 128 + 128].astype(F32)
                for h in range(LOCAL_HEADS)
            )

        zero = jnp.zeros((HEAD_DIM, HEAD_DIM), F32)
        carried = lax.fori_loop(0, zy, advance, (zero,) * LOCAL_HEADS)
        first = whole(sx.at[0], 512)
        return [
            jnp.where(
                c == 0, carried[h],
                first[h : h + 1] * carried[h] + sx[0, h * 128 : h * 128 + 128].astype(F32),
            )
            for h in range(LOCAL_HEADS)
        ]

    def student(pieces, incoming, h):
        for i in range(2):
            reach = jnp.exp(pieces[i][1]) * SCALE
            state = incoming[h] if i == 0 else pieces[0][3][h : h + 1] * incoming[h] + contrib[0, h]
            carried = dot(ct[h, rows_of[i]], state.astype(BF))
            out = inner[h, rows_of[i]] + reach[:, h : h + 1] * carried
            student_ref[rows_of[i], h * 128 : h * 128 + 128] = out.astype(BF)

    ones = jnp.ones((16, TOK), BF)

    def absorb(blocks, heads, diagonal=False):
        todo = [(b, h, i) for b in range(len(blocks)) for h in heads for i in range(TOK // HALF)]

        def reach_of(i):
            return (i + 1) * HALF if diagonal else TOK

        def scores(n):
            b, h, i = todo[n]
            keys = kall[(*blocks[b],)]
            keys = jnp.concatenate(
                [keys[:, k * 128 : k * 128 + 128] for k in range(reach_of(i) // 128)], axis=0
            )
            out = dot_t(keys, rq[h, i * HALF : i * HALF + HALF])
            if diagonal:
                at_u = lax.broadcasted_iota(jnp.int32, out.shape, 0)
                at_t = lax.broadcasted_iota(jnp.int32, out.shape, 1) + i * HALF
                out = jnp.where(at_u <= at_t, out, FAR_BELOW)
            return out

        found = {n: scores(n) for n in range(min(2, len(todo)))}
        ready = None
        for n in range(len(todo) + 1):
            now = None
            if n + 2 < len(todo):
                found[n + 2] = scores(n + 2)
            if n < len(todo):
                b, h, i = todo[n]
                cols = slice(i * HALF, i * HALF + HALF)
                score = found.pop(n)
                high = jnp.max(score, axis=0, keepdims=True)
                if diagonal:
                    peak, shrink = high, None
                else:
                    before = top[h, 0:1, cols]
                    peak = jnp.maximum(before, high)
                    shrink = jnp.exp2(before - peak)
                now = (b, h, cols, jnp.exp2(score - peak).astype(BF), shrink)
                top[h, 0:1, cols] = peak
            if ready is not None:
                b, h, cols, weights, shrink = ready
                seen = weights.shape[0]
                wide = jnp.concatenate([vall[(*blocks[b],)][:, :seen], ones[:, :seen]], axis=0)
                mixed = dot(wide, weights)
                acc[h, :, cols] = mixed if diagonal else mixed + acc[h, :, cols] * shrink
            ready = now

    def own_part(heads, part):
        if part == 0:
            absorb([(c, zy)], heads, True)
            return
        if part == 1:
            pl.when(c == 1)(lambda: absorb([(0, zy)], heads))
            return

        if len(heads) > 1:

            def visit(j, carry):
                absorb([(0, j), (1, j)], heads)
                return carry

            lax.fori_loop(zh * 4, zy, visit, 0)
            return
        first, chips = zh * 4, p["y"]
        pl.when(chips >= 2)(lambda: absorb([(k % 2, first + k // 2) for k in range(4)], heads))
        last = zy - 1
        pl.when(chips % 2 == 1)(lambda: absorb([(0, last), (1, last)], heads))

    def low_part(heads, part):
        if len(heads) > 1:
            blocks = [(k % 2, part * 2 + k // 2) for k in range(4)]
        else:
            blocks = [(k % 2, k // 2) for k in range(8)]
        pl.when(zh == 1)(lambda: absorb(blocks, heads))

    def teacher(h):
        done = acc[h]
        out = (done[:128] / done[128:129]).T
        teacher_ref[:, h * 128 : h * 128 + 128] = out.astype(BF)

    for cp in x_copies():
        cp.start()
    place("k")
    enter(["R", "L", "Z", "S", "G"], p)
    w["k"].ay()
    w["k"].az()
    arrange()
    send_raw()
    place("v")
    w["v"].ay()
    place("q0")
    w["q0"].ay()
    w["k"].f()
    place("q3")
    w["v"].az()
    w["v"].f()
    w["q3"].ay()
    w["k"].zs()
    w["q0"].az()
    w["k"].s1()
    w["q0"].f()
    w["v"].s1()
    w["v"].zs()
    w["k"].zf()
    w["q3"].f()
    place("q1")
    w["q1"].ay()
    w["q1"].az()
    w["q0"].s1()
    w["v"].zf()
    w["k"].s2()
    w["q3"].s1()
    place("q2")
    w["q0"].zs()
    w["q2"].az()
    w["q2"].ay()
    multiply("k")
    pieces = decays()
    w["v"].s2()
    w["q0"].zf()
    w["q1"].zs()
    w["q3"].az()
    w["q1"].f()
    multiply("v")
    w["q2"].f()
    w["q0"].s2()
    w["q1"].zf()
    w["q2"].zs()
    w["q1"].s1()
    settle("k")
    kept["k"].a()
    multiply("q0")
    w["q2"].s1()
    w["q1"].s2()
    settle("v")
    local_state(pieces)
    w["q2"].zf()
    w["q3"].zs()
    kept["v"].a()
    multiply("q1")
    w["q2"].s2()
    w["q3"].zf()
    kept["k"].b()
    settle("q0")
    multiply("q2")
    kept["v"].b()
    kept["k"].zs()
    chip_state()
    kept["s"].a()
    kept["v"].zs()
    inside(pieces, 0)
    w["q3"].s2()
    kept["k"].c()
    kept["v"].c()
    settle("q1")
    own_part([0, 1], 0)
    multiply("q3")
    kept["k"].near()
    kept["s"].zs()
    inside(pieces, 1)
    kept["k"].zf()
    kept["v"].near()
    own_part([0, 1], 2)
    kept["v"].zf()
    kept["s"].b()
    settle("q2")
    inside(pieces, 2)
    own_part([2], 0)
    own_part([2], 1)
    kept["k"].d()
    kept["s"].zf()
    own_part([2], 2)
    own_part([0, 1], 1)
    kept["v"].d()
    kept["s"].d()
    settle("q3")
    own_part([3], 0)
    inside(pieces, 3)
    kept["k"].e()
    kept["s"].c()
    own_part([3], 2)
    kept["v"].e()
    low_part([0, 1], 1)
    low_part([0, 1], 0)
    teacher(0)
    kept["s"].near()
    kept["s"].e()
    own_part([3], 1)
    incoming = arriving()
    student(pieces, incoming, 3)
    student(pieces, incoming, 2)
    low_part([2], 1)
    student(pieces, incoming, 1)
    low_part([3], 1)
    teacher(2)
    student(pieces, incoming, 0)
    teacher(3)
    teacher(1)
    for name in KINDS:
        w[name].sent()
        for cp in tiles(name):
            cp.wait_send()
    for d in range(3):
        raw_tile(d).wait_send()
    for name in kept:
        kept[name].sent()
    swap().wait_send()


def tables():
    half = HEAD_DIM // 2
    freq = ROPE_BASE ** (-2.0 * np.arange(half) / HEAD_DIM)
    freq = np.concatenate([freq, freq])
    near = np.arange(TOK)[:, None] * freq[None]
    base = (np.arange(16) * TOK)[:, None] * freq[None]
    return (
        np.stack([np.cos(near), np.sin(near)]).astype(np.float32),
        np.stack([np.cos(base), np.sin(base)]).astype(np.float32),
    )


def hand_over_kernel(teacher_ref, student_ref, teacher_out, student_out):
    teacher_out[...] = teacher_ref[...]
    student_out[...] = student_ref[...]


def body(layer_input, attn_weight, rate_weight, rate_bias, decay_rate, skip_gain):
    vmem = pl.BlockSpec(memory_space=pltpu.VMEM)
    smem = pl.BlockSpec(memory_space=pltpu.SMEM)
    dma = pltpu.SemaphoreType.DMA
    near, base = tables()
    heads = (LOCAL_HEADS, TOK, HEAD_DIM)
    results = pl.pallas_call(
        window_kernel,
        name="window",
        out_shape=(
            jax.ShapeDtypeStruct((TOK, 512), BF),
            jax.ShapeDtypeStruct((TOK, 512), BF),
        ),
        in_specs=[pl.BlockSpec(memory_space=pl.ANY)] + [vmem] * 4 + [smem] * 3,
        out_specs=(vmem, vmem),
        scratch_shapes=[
            pltpu.VMEM((2, 2, 8, 128, 256), BF),
            pltpu.VMEM((4, 2, 8, 128, 512), BF),
            pltpu.VMEM((2, TOK, 1024), BF),
            pltpu.VMEM((2, 2, TOK, 128), F32),
            pltpu.VMEM((2, 4, TOK, 128), F32),
            pltpu.VMEM((4, 4, TOK, 128), BF),
            pltpu.VMEM((4, 3, TOK, 128), BF),
            pltpu.VMEM((2, 2, TOK, 128), BF),
            pltpu.VMEM((2, 3, TOK, 128), BF),
            pltpu.VMEM((4, 8, TOK), F32),
            pltpu.VMEM((3, 8, TOK), F32),
            pltpu.VMEM((2, 8, 128, TOK), BF),
            pltpu.VMEM((2, 8, 128, TOK), BF),
            pltpu.VMEM((2, 8, 272, 128), BF),
            pltpu.VMEM((2, 528, 128), BF),
            pltpu.VMEM(heads, BF),
            pltpu.VMEM(heads, BF),
            pltpu.VMEM((TOK, HEAD_DIM), BF),
            pltpu.VMEM((TOK, HEAD_DIM), BF),
            pltpu.VMEM((2, LOCAL_HEADS, HEAD_DIM, HEAD_DIM), F32),
            pltpu.VMEM(heads, F32),
            pltpu.VMEM((LOCAL_HEADS, 144, TOK), F32),
            pltpu.VMEM((LOCAL_HEADS, 8, TOK), F32),
            dma((len(KINDS), COPIES)),
            dma((len(KINDS), COPIES)),
            dma((len(KINDS) + 1, 3)),
            dma((len(KINDS) + 1, 3)),
            dma((3, COPIES)),
            dma((3, COPIES)),
            dma,
            dma,
            dma((16,)),
        ],
        compiler_params=pltpu.CompilerParams(
            collective_id=0, has_side_effects=True, vmem_limit_bytes=58 * 2**20
        ),
    )(
        layer_input, attn_weight, rate_weight.T, jnp.asarray(near),
        jnp.asarray(base), rate_bias, decay_rate, skip_gain,
    )
    half = pl.BlockSpec((TOK // 2, 512), lambda i: (i, 0))
    return pl.pallas_call(
        hand_over_kernel,
        name="hand_over",
        grid=(2,),
        out_shape=(jax.ShapeDtypeStruct((TOK, 512), BF),) * 2,
        in_specs=[half] * 2,
        out_specs=(half,) * 2,
    )(*results)


def solution(mesh):
    placed = (
        P("seq", "grp"),
        P(("grp", "seq"), "mdl", None),
        P("grp", "mdl"),
        P(("mdl", "grp")),
        P(("mdl", "grp")),
        P(("mdl", "grp")),
    )
    return jax.shard_map(
        body,
        mesh=mesh,
        in_specs=placed,
        out_specs=(P("seq", ("mdl", "grp")), P("seq", ("mdl", "grp"))),
        check_vma=False,
    )
```
